32 devices in a mesh: parts: 2 (over y), ctx: 4 (over z), opt: 4 (over x, core).
Axes of the slice: x: 2, y: 2, z: 4, core: 2. Of those that a mesh axis runs over, the one named last changes fastest.
Arguments:
- options: bfloat16 [8, 32, 3072], P(('parts', 'opt'), 'ctx'), parts along dimension 0, may hold values from -6 to 6
- cache_keys: bfloat16 [1024, 512], P(('parts', 'ctx')), parts along dimension 0, may hold values from -800 to 800
- cache_values: bfloat16 [1024, 512], P(('parts', 'ctx')), parts along dimension 0, may hold values from -6 to 6
- attention_gain: float32 [3072], replicated, may hold values from 0.5 to 1.5
- expert_gain: float32 [3072], replicated, may hold values from 0.5 to 1.5
- input_weight: bfloat16 [3072, 4096], P(None, 'ctx'), may hold values from -0.109375 to 0.109375
- output_weight: bfloat16 [3072, 3072], P(None, 'ctx'), may hold values from -0.875 to 0.875
- router_weight: bfloat16 [3072, 8], replicated, may hold values from -0.109375 to 0.109375
- gate_weight: bfloat16 [3072, 65536], P(None, ('ctx', 'opt')), may hold values from -0.109375 to 0.109375
- up_weight: bfloat16 [3072, 65536], P(None, ('ctx', 'opt')), may hold values from -0.109375 to 0.109375
- down_weight: bfloat16 [65536, 3072], P(('ctx', 'opt')), may hold values from -0.0625 to 0.0625
- routing: int32 [8, 32, 2], P(('parts', 'opt'), 'ctx'), parts along dimension 0, may hold values from 0 to 7, all different within a row; in each aligned block of 8 rows (0 to 7, 8 to 15, ..., all dimensions but the last counted through in order) at most 4 rows name the same one
Outputs:
- layer_out: bfloat16 [8, 32, 3072], P(('parts', 'opt'), 'ctx'), parts along dimension 0
The draws below stay inside these ranges and needn't reach their ends.
There are 2 independent parts, one for each index of `parts`. The reference program is written for one: setup_inputs(seed, part) draws one part's arguments, and reference() takes and returns one part's arrays. A program takes and returns all parts, laid end to end along the dimension named above; an argument that names none is the same for every part. Nothing has to cross between parts.
Inputs may be any that keep to these rules, and one draw needn't show every extreme that they name: `routing`: at most 4 of the 8 rows of one device name the same expert, and in some device one expert is named by exactly 4 rows; the two experts of a row differ.
All inputs are finite; a program needn't handle non-finite values.
Results may differ from the reference program's by a relative error of at most 0.018.
Values may be sent and summed in bfloat16 or wider, within the bound.
No kernel may reach another device: no remote copies, remote signals or barrier semaphores. Data moves between devices by JAX's collectives and lax.ppermute only.
A program may use at most 192 MiB of HBM per device.

```python
import math
import jax
import jax.numpy as jnp
import numpy as np
from jax import lax

D = 3072
H = 24
KVH = 4
HD = 128
E = 8
FF = 8192
TOPK = 2
PASS_DEV = 128
OT_DEV = 8
G = 6
PASSAGE = 512
OPT_LEN = 32
MOST = 4
N_CTX = 4
N_OPT = 4


def draw_cache_keys(key, part):
    base = jax.random.normal(key, (PASSAGE, KVH * HD), jnp.float32)
    return jnp.clip(base, -6.0, 6.0).astype(jnp.bfloat16)


def block_levels(stream_key, shape, cuts, low, high):
    def one(axis_at, blocks):
        heights = jax.random.uniform(jax.random.fold_in(jax.random.fold_in(stream_key, 6), axis_at), (blocks,), jnp.float32, low / len(cuts), high / len(cuts))
        return jnp.repeat(jnp.exp(heights), shape[axis_at] // blocks).reshape((-1,) + (1,) * (len(shape) - axis_at - 1))

    gain = one(*cuts[0])
    for cut in cuts[1:]:
        gain = gain * one(*cut)
    return gain


def deal_out(stream_key, own, number, rows, count, top, most, skew):
    order = jax.random.permutation(stream_key, count)
    heavy_load, usual = shares(count, rows * top, most, skew, True), shares(count, rows * top, most, skew, False)
    places = jnp.arange(count)

    def named(lengths, turn):
        used = int((lengths > 0).sum())
        fixed = max(1, used // 4)
        passed = fixed + (places - fixed + turn * (used - fixed)) % max(1, count - fixed)
        return jnp.zeros((count,), jnp.int32).at[order[jnp.where(places < fixed, places, passed)]].set(jnp.asarray(lengths, jnp.int32))

    lengths = jnp.where(number % 4 == 0, named(heavy_load, number // 4), named(usual, number - number // 4 - 1))
    mixed = jax.random.permutation(jax.random.fold_in(own, 3), count)
    giver, sink = mixed[0:count // 2 * 2:2], mixed[1:count // 2 * 2:2]
    margin = jnp.minimum(lengths[giver] - 1, most - lengths[sink]) // 2
    margin = jnp.where((giver == order[0]) | (sink == order[0]) | (lengths[sink] == 0), 0, jnp.maximum(margin, 0))
    passed = jax.random.randint(jax.random.fold_in(own, 4), (count // 2,), 0, 1 << 20) % (margin + 1)
    lengths = lengths.at[giver].add(-passed).at[sink].add(passed)
    members = jnp.searchsorted(jnp.cumsum(lengths), jnp.arange(rows * top), side="right").astype(jnp.int32)
    listing = members.reshape(top, rows).T
    listing = listing[jax.random.permutation(jax.random.fold_in(own, 1), rows)]
    turn = jax.random.randint(jax.random.fold_in(own, 2), (rows, 1), 0, top)
    return jnp.take_along_axis(listing, (jnp.arange(top)[None, :] + turn) % top, axis=1)


def shares(count, total, limit, lean, full):
    loads = [(1 << 20) // math.isqrt(grade ** lean) + 1 for grade in range(1, count + 1)]
    largest = limit if full else min(limit, max(-(-total // count), total * loads[0] // sum(loads)))
    least = 1 if total - largest >= count - 1 else 0
    counts, rest = [largest] + [least] * (count - 1), total - largest - least * (count - 1)
    while rest > 0:
        candidates = [i for i in range(1, count) if counts[i] < largest] or [i for i in range(1, count) if counts[i] < limit]
        mass, left = sum([loads[i] for i in candidates]), rest
        for i in candidates:
            extra = min(limit - counts[i], max(1, left * loads[i] // mass), rest)
            counts[i] = counts[i] + extra
            rest = rest - extra
    return np.array(counts)


def scatter_about(own_key, dims, width, bound, cuts=(), held_as=jnp.bfloat16):
    factor_of = block_levels(own_key, dims, cuts, -0.22, 0.18) if cuts else 1.0
    entries = jax.random.normal(own_key, dims, jnp.float32) * width * factor_of
    return jnp.minimum(jnp.maximum(entries, -bound), bound).astype(held_as)


def setup_inputs(seed: int = 0, part: int = 0) -> dict:
    arg_keys = jax.random.split(jax.random.key(seed), 13)
    part_keys = jax.random.split(jax.random.fold_in(arg_keys[12], part), 13)
    options = scatter_about(part_keys[0], (N_OPT, OPT_LEN, D), 1.0, 6.0, ((0, 4), (1, 4)))
    cache_keys = draw_cache_keys(jax.random.fold_in(jax.random.fold_in(arg_keys[12], part), 71), part)
    cache_values = scatter_about(part_keys[2], (PASSAGE, KVH * HD), 1.0, 6.0, ((0, 4),))
    attention_gain = jnp.clip(1.0 + 0.1 * jax.random.normal(arg_keys[3], (D,), jnp.float32), 0.5, 1.5)
    expert_gain = jnp.clip(1.0 + 0.1 * jax.random.normal(arg_keys[4], (D,), jnp.float32), 0.5, 1.5)
    input_weight = scatter_about(arg_keys[5], (D, (H + 2 * KVH) * HD), D ** -0.5, 0.109375, ((1, 4),))
    output_weight = scatter_about(arg_keys[6], (H * HD, D), (max(1, H * HD * 8 // (PASS_DEV * N_CTX + OT_DEV * N_CTX))) ** -0.5, 0.875, ((1, 4),))
    router_weight = scatter_about(arg_keys[7], (D, E), D ** -0.5, 0.109375)
    gate_weight = scatter_about(arg_keys[8], (D, E * FF), D ** -0.5, 0.109375, ((1, 16),))
    up_weight = scatter_about(arg_keys[9], (D, E * FF), D ** -0.5, 0.109375, ((1, 16),))
    down_weight = scatter_about(arg_keys[10], (E * FF, D), FF ** -0.5, 0.0625, ((0, 16),))
    routing_keys = jax.random.split(jax.random.fold_in(part_keys[11], 1), N_OPT * OPT_LEN // OT_DEV)
    routing_turns = jax.random.permutation(jax.random.fold_in(part_keys[11], 3), N_OPT * OPT_LEN // OT_DEV)
    routing = jax.vmap(lambda own, number: deal_out(jax.random.fold_in(part_keys[11], 2), own, number, OT_DEV, E, TOPK, MOST, 2))(routing_keys, routing_turns).reshape((N_OPT, OPT_LEN, TOPK))
    return {"options": options, "cache_keys": cache_keys, "cache_values": cache_values, "attention_gain": attention_gain, "expert_gain": expert_gain, "input_weight": input_weight, "output_weight": output_weight, "router_weight": router_weight, "gate_weight": gate_weight, "up_weight": up_weight, "down_weight": down_weight, "routing": routing}


EPS = 1e-05
THETA = 1000000.0

def rms_scale(row_data, gain_vector):
    floats = row_data.astype(jnp.float32)
    factor = lax.rsqrt(lax.optimization_barrier(jnp.mean(floats * floats, axis=-1, keepdims=True)) + EPS)
    return (floats * factor * gain_vector).astype(jnp.bfloat16)

def rotate(tile_data, first_head, positions):
    row_count, tile_width = tile_data.shape
    head_count = tile_width // HD
    half_dim = HD // 2
    split_view = tile_data.reshape(row_count, head_count, 2, half_dim)
    inverse = THETA ** (-2.0 * jnp.arange(half_dim, dtype=jnp.float32) / HD)
    angles = positions.astype(jnp.float32)[:, None] * inverse[None, :]
    cosine = jnp.cos(angles)[:, None, :]
    sine_part = jnp.sin(angles)[:, None, :]
    lower_half = split_view[:, :, 0]
    upper_half = split_view[:, :, 1]
    turned = jnp.stack([lower_half * cosine - upper_half * sine_part, upper_half * cosine + lower_half * sine_part], axis=2)
    rotated_head = first_head + jnp.arange(head_count) < H + KVH
    return jnp.where(rotated_head[None, :, None, None], turned, split_view).reshape(row_count, tile_width)

def softmax_parts(queries, key_rows, value_rows, query_start, key_start, cached):
    key_count = key_rows.shape[0]
    key_heads = key_rows.reshape(key_count, KVH, HD).astype(jnp.float32)
    value_heads = value_rows.reshape(key_count, KVH, HD).astype(jnp.float32)
    scores = jnp.einsum('rhgd,khd->hgrk', queries.astype(jnp.float32), key_heads, precision=lax.Precision.HIGHEST) * HD ** (-0.5)
    query_index = query_start + jnp.arange(queries.shape[0])
    key_index = jnp.arange(key_count)
    visible = (key_index[None, :] < cached) | (key_start + key_index[None, :] - cached <= query_index[:, None])
    scores = jnp.where(visible, scores, -jnp.inf)
    maxima = lax.optimization_barrier(jnp.max(scores, axis=-1))
    weights = jnp.exp(scores - maxima[..., None])
    totals = lax.optimization_barrier(jnp.sum(weights, axis=-1))
    summed = jnp.einsum('hgrk,khd->hgrd', weights, value_heads, precision=lax.Precision.HIGHEST)
    return (maxima, totals, summed)

def reference(options, cache_keys, cache_values, attention_gain, expert_gain, input_weight, output_weight, router_weight, gate_weight, up_weight, down_weight, routing):
    positions = PASSAGE + jnp.arange(OPT_LEN)
    query_width = H * HD
    key_end = (H + KVH) * HD
    mixed_list = []
    for option in range(N_OPT):
        own_rows = options[option]
        normed = rms_scale(own_rows, attention_gain)
        projected = jnp.dot(normed, input_weight, preferred_element_type=jnp.float32)
        rotated = rotate(projected, 0, positions).astype(jnp.bfloat16)
        queries = rotated[:, :query_width].reshape(OPT_LEN, KVH, G, HD)
        key_rows = jnp.concatenate([cache_keys, rotated[:, query_width:key_end]], axis=0)
        value_rows = jnp.concatenate([cache_values, rotated[:, key_end:]], axis=0)
        maxima, totals, summed = softmax_parts(queries, key_rows, value_rows, 0, 0, PASSAGE)
        attention = (summed / totals[..., None]).transpose(2, 0, 1, 3).reshape(OPT_LEN, query_width).astype(jnp.bfloat16)
        attention_out = jnp.dot(attention, output_weight, preferred_element_type=jnp.float32).astype(jnp.bfloat16)
        mixed_list.append((own_rows.astype(jnp.float32) + attention_out.astype(jnp.float32)).astype(jnp.bfloat16))
    mixed_in = jnp.stack(mixed_list).reshape(N_OPT * OPT_LEN, D)
    expert_in = rms_scale(mixed_in, expert_gain)
    chosen_ids = routing.reshape(N_OPT * OPT_LEN, TOPK)
    logits = jnp.dot(expert_in, router_weight, preferred_element_type=jnp.float32)
    picked = jnp.take_along_axis(logits, chosen_ids, axis=1)
    gate_share = jax.nn.softmax(picked, axis=-1)
    token_total = N_OPT * OPT_LEN
    capacity = min(token_total, N_OPT * N_CTX * MOST)
    serial = jnp.arange(token_total, dtype=jnp.int32)
    expert_sum = jnp.zeros((token_total, D), jnp.float32)
    for expert in range(E):
        named_here = chosen_ids == expert
        token_share = lax.optimization_barrier(jnp.sum(jnp.where(named_here, gate_share, 0.0), axis=1))
        sort_key = jnp.where(jnp.any(named_here, axis=1), 0, token_total).astype(jnp.int32) + serial
        picked_rows = jnp.argsort(sort_key)[:capacity].astype(jnp.int32)
        taken_rows = expert_in[picked_rows]
        column_start = expert * FF
        gate_part = jnp.dot(taken_rows, gate_weight[:, column_start:column_start + FF], preferred_element_type=jnp.float32)
        up_part = jnp.dot(taken_rows, up_weight[:, column_start:column_start + FF], preferred_element_type=jnp.float32)
        hidden = (jax.nn.silu(gate_part) * up_part).astype(jnp.bfloat16)
        result = jnp.dot(hidden, down_weight[column_start:column_start + FF], preferred_element_type=jnp.float32)
        expert_sum = expert_sum.at[picked_rows].add(result * token_share[picked_rows][:, None])
    layer_out = (mixed_in.astype(jnp.float32) + expert_sum).astype(jnp.bfloat16)
    return layer_out.reshape(N_OPT, OPT_LEN, D)
```

```python
import jax
import jax.numpy as jnp
from jax import lax
from jax.experimental import pallas as pl
from jax.experimental.pallas import tpu as pltpu
from jax.sharding import PartitionSpec as P

H = 24
KVH = 4
HD = 128
FF = 8192
MOST = 4


EPS = 1e-05
THETA = 1000000.0


def combined_all(x, axis, combine):
    everything = jax.tree.map(
        lambda part, kind: lax.all_gather(part.astype(kind), axis),
        x,
        (jnp.bfloat16, jnp.bfloat16, jnp.bfloat16),
    )

    def take(k):
        return jax.tree.map(lambda part, own: part[k].astype(own.dtype), everything, x)

    return lax.fori_loop(
        1, lax.axis_size(axis), lambda k, so_far: combine(so_far, take(k)), take(0)
    )


def rms_scale(row_data, gain_vector):
    floats = row_data.astype(jnp.float32)
    factor = lax.rsqrt(jnp.mean(floats * floats, axis=-1, keepdims=True) + EPS)
    return (floats * factor * gain_vector).astype(jnp.bfloat16)


def rotate(tile_data, first_head, positions):
    row_count, tile_width = tile_data.shape
    head_count = tile_width // HD
    half_dim = HD // 2
    split_view = tile_data.reshape(row_count, head_count, 2, half_dim)
    inverse = THETA ** (-2.0 * jnp.arange(half_dim, dtype=jnp.float32) / HD)
    angles = positions.astype(jnp.float32)[:, None] * inverse[None, :]
    cosine = jnp.cos(angles)[:, None, :]
    sine_part = jnp.sin(angles)[:, None, :]
    lower_half = split_view[:, :, 0]
    upper_half = split_view[:, :, 1]
    turned = jnp.stack(
        [
            lower_half * cosine - upper_half * sine_part,
            upper_half * cosine + lower_half * sine_part,
        ],
        axis=2,
    )
    rotated_head = first_head + jnp.arange(head_count) < H + KVH
    return jnp.where(rotated_head[None, :, None, None], turned, split_view).reshape(
        row_count, tile_width
    )


def softmax_parts(queries, key_rows, value_rows, key_start, cached):
    key_count = key_rows.shape[0]
    key_heads = key_rows.reshape(key_count, KVH, HD)
    value_heads = value_rows.reshape(key_count, KVH, HD).astype(jnp.float32)
    scores = jnp.einsum(
        "rhgd,khd->hgrk", queries, key_heads, preferred_element_type=jnp.float32
    ) * HD ** (-0.5)
    query_index = jnp.arange(queries.shape[0])
    key_index = jnp.arange(key_count)
    visible = (key_index[None, :] < cached) | (
        key_start + key_index[None, :] - cached <= query_index[:, None]
    )
    scores = jnp.where(visible, scores, -jnp.inf)
    maxima = jnp.max(scores, axis=-1)
    weights = jnp.exp(scores - maxima[..., None])
    totals = jnp.sum(weights, axis=-1)
    summed = jnp.einsum("hgrk,khd->hgrd", weights, value_heads, precision=lax.Precision.HIGHEST)
    return (maxima, totals, summed)


def join_parts(first, second):
    first_max, first_total, first_sum = first
    second_max, second_total, second_sum = second
    larger = jnp.maximum(first_max, second_max)
    first_scale = jnp.exp(first_max - larger)
    second_scale = jnp.exp(second_max - larger)
    return (
        larger,
        first_total * first_scale + second_total * second_scale,
        first_sum * first_scale[..., None] + second_sum * second_scale[..., None],
    )


def general_shards(
    options,
    cache_keys,
    cache_values,
    attention_gain,
    expert_gain,
    input_weight,
    output_weight,
    router_weight,
    gate_weight,
    up_weight,
    down_weight,
    routing,
):
    own_rows = options[0]
    ctx_count = lax.axis_size("ctx")
    ctx_here = lax.axis_index("ctx")
    local_rows = own_rows.shape[0]
    passage = cache_keys.shape[0] * ctx_count
    tile_columns = input_weight.shape[1]
    first_head = ctx_here * (tile_columns // HD)
    normed = rms_scale(own_rows, attention_gain)
    row_piece = lax.all_gather(normed, "ctx", axis=0, tiled=True)
    product = jnp.dot(row_piece, input_weight, preferred_element_type=jnp.float32)
    where_at = passage + jnp.int32(0) + jnp.arange(row_piece.shape[0])
    rotated_tile = rotate(product, first_head, where_at).astype(jnp.bfloat16)
    projected = lax.all_gather(rotated_tile, "ctx", axis=1, tiled=True)
    option_len = projected.shape[0]
    query_width = H * HD
    key_end = (H + KVH) * HD
    queries = projected[:, :query_width].reshape(option_len, KVH, H // KVH, HD)
    option_keys = projected[:, query_width:key_end]
    option_values = projected[:, key_end:]
    own_start = ctx_here * local_rows
    own_keys = lax.dynamic_slice_in_dim(option_keys, own_start, local_rows, 0)
    own_values = lax.dynamic_slice_in_dim(option_values, own_start, local_rows, 0)
    key_rows = jnp.concatenate([cache_keys, own_keys], axis=0)
    value_rows = jnp.concatenate([cache_values, own_values], axis=0)
    local_max, local_total, local_sum = softmax_parts(
        queries, key_rows, value_rows, own_start, cache_keys.shape[0]
    )
    maxima, totals, summed = combined_all((local_max, local_total, local_sum), "ctx", join_parts)
    attention = (
        (summed / totals[..., None])
        .transpose(2, 0, 1, 3)
        .reshape(option_len, query_width)
        .astype(jnp.bfloat16)
    )
    columns = jnp.dot(attention, output_weight, preferred_element_type=jnp.float32).astype(
        jnp.bfloat16
    )
    attention_out = lax.all_to_all(columns, "ctx", split_axis=0, concat_axis=1, tiled=True)
    mixed_in = (own_rows.astype(jnp.float32) + attention_out.astype(jnp.float32)).astype(
        jnp.bfloat16
    )
    expert_in = rms_scale(mixed_in, expert_gain)
    chosen_ids = routing[0]
    top_count = chosen_ids.shape[1]
    expert_count = router_weight.shape[1]
    logits = jnp.dot(expert_in, router_weight, preferred_element_type=jnp.float32)
    matches = chosen_ids[:, :, None] == jnp.arange(expert_count)[None, None, :]
    picked = jnp.sum(jnp.where(matches, logits[:, None, :], 0.0), axis=-1)
    gate_share = jax.nn.softmax(picked, axis=-1)
    ctx_width = expert_count * FF // ctx_count
    first_target = chosen_ids * FF // ctx_width
    last_target = ((chosen_ids + 1) * FF - 1) // ctx_width
    destination = jnp.arange(ctx_count)
    goes_to = (destination[None, None, :] >= first_target[:, :, None]) & (
        destination[None, None, :] <= last_target[:, :, None]
    )
    flat_goes = goes_to.reshape(local_rows * top_count, ctx_count).astype(jnp.int32)
    slot_index = jnp.cumsum(flat_goes, axis=0) - flat_goes
    slot_count = MOST * max(1, expert_count // ctx_count)
    slot_match = (flat_goes[:, :, None] == 1) & (
        slot_index[:, :, None] == jnp.arange(slot_count)[None, None, :]
    )
    slot_match = slot_match.reshape(local_rows, top_count, ctx_count * slot_count)
    token_slots = jnp.any(slot_match, axis=1).astype(jnp.bfloat16)
    model_width = expert_in.shape[1]
    outgoing = jnp.einsum(
        "rs,rd->sd", token_slots, expert_in, preferred_element_type=jnp.float32
    ).astype(jnp.bfloat16)
    outgoing = outgoing.reshape(ctx_count, slot_count, model_width)
    outgoing_ids = jnp.sum(jnp.where(slot_match, chosen_ids[:, :, None] + 1, 0), axis=(0, 1)) - 1
    outgoing_ids = outgoing_ids.reshape(ctx_count, slot_count)
    arrived, arrived_ids = (
        lax.all_to_all(outgoing, "ctx", split_axis=0, concat_axis=0, tiled=True),
        lax.all_to_all(outgoing_ids, "ctx", split_axis=0, concat_axis=0, tiled=True),
    )
    pooled, pooled_ids = (
        lax.all_gather(arrived, "opt", axis=0, tiled=True),
        lax.all_gather(arrived_ids, "opt", axis=0, tiled=True),
    )
    pooled = pooled.reshape(-1, model_width)
    pooled_ids = pooled_ids.reshape(-1)
    local_width = gate_weight.shape[1]
    opt_count = lax.axis_size("opt")
    column_start = (ctx_here * opt_count + lax.axis_index("opt")) * local_width
    column_expert = (column_start + jnp.arange(local_width)) // FF
    owned_mask = pooled_ids[:, None] == column_expert[None, :]
    gate_part = jnp.dot(pooled, gate_weight, preferred_element_type=jnp.float32)
    up_part = jnp.dot(pooled, up_weight, preferred_element_type=jnp.float32)
    hidden = jnp.where(owned_mask, jax.nn.silu(gate_part) * up_part, 0.0).astype(jnp.bfloat16)
    partial_out = jnp.dot(hidden, down_weight, preferred_element_type=jnp.float32)
    summed_back = lax.psum_scatter(
        partial_out.astype(jnp.bfloat16), "opt", scatter_dimension=0, tiled=True
    ).astype(jnp.float32)
    returned = lax.all_to_all(
        summed_back.reshape(ctx_count, slot_count, model_width).astype(jnp.bfloat16),
        "ctx",
        split_axis=0,
        concat_axis=0,
        tiled=True,
    ).astype(jnp.float32)
    weighting = jnp.sum(jnp.where(slot_match, gate_share[:, :, None], 0.0), axis=1)
    expert_sum = jnp.dot(
        weighting,
        returned.reshape(-1, model_width),
        precision=lax.Precision.HIGHEST,
        preferred_element_type=jnp.float32,
    )
    layer_out = (mixed_in.astype(jnp.float32) + expert_sum).astype(jnp.bfloat16)
    return layer_out[None]


def gate_up_kernel(rows_ref, gate_ref, up_ref, hidden_ref):
    gate = jnp.dot(rows_ref[...], gate_ref[...], preferred_element_type=jnp.float32)
    up = jnp.dot(rows_ref[...], up_ref[...], preferred_element_type=jnp.float32)
    hidden_ref[...] = (gate / (1.0 + jnp.exp(-gate)) * up).astype(hidden_ref.dtype)


def down_kernel(hidden_ref, down_ref, out_ref):
    out_ref[...] = jnp.dot(
        hidden_ref[...], down_ref[...], preferred_element_type=jnp.float32
    ).astype(out_ref.dtype)


def tile_of(columns, most=1024):
    tile = most
    while columns % tile:
        tile //= 2
    return tile


def expert_hidden(rows, gate_weight, up_weight):
    count, depth = rows.shape
    columns = gate_weight.shape[1]
    tile = tile_of(columns)
    weight_spec = pl.BlockSpec((depth, tile), lambda j: (0, j))
    return pl.pallas_call(
        gate_up_kernel,
        out_shape=jax.ShapeDtypeStruct((count, columns), jnp.bfloat16),
        grid=(columns // tile,),
        in_specs=[pl.BlockSpec((count, depth), lambda j: (0, 0)), weight_spec, weight_spec],
        out_specs=pl.BlockSpec((count, tile), lambda j: (0, j)),
        cost_estimate=pl.CostEstimate(
            flops=4 * count * depth * columns,
            bytes_accessed=4 * depth * columns,
            transcendentals=count * columns,
        ),
        name="expert_hidden",
    )(rows, gate_weight, up_weight)


def expert_down(hidden, down_weight, kind):
    count, depth = hidden.shape
    columns = down_weight.shape[1]
    tile = tile_of(columns)
    return pl.pallas_call(
        down_kernel,
        out_shape=jax.ShapeDtypeStruct((count, columns), kind),
        grid=(columns // tile,),
        in_specs=[
            pl.BlockSpec((count, depth), lambda j: (0, 0)),
            pl.BlockSpec((depth, tile), lambda j: (0, j)),
        ],
        out_specs=pl.BlockSpec((count, tile), lambda j: (0, j)),
        cost_estimate=pl.CostEstimate(
            flops=2 * count * depth * columns,
            bytes_accessed=2 * depth * columns,
            transcendentals=0,
        ),
        name="expert_down",
    )(hidden, down_weight)


def flip(x, axis, mask):
    return lax.ppermute(x, axis, [(i, i ^ mask) for i in range(lax.axis_size(axis))])


def by_index(index, variants):
    chosen = variants[0]
    for k in range(1, len(variants)):
        chosen = jnp.where(index == k, variants[k], chosen)
    return chosen


def gathered(x, axis, index):
    count = lax.axis_size(axis)
    parts = [x] + [None] * (count - 1)
    for mask in range(count - 1, 0, -1):
        parts[mask] = flip(x, axis, mask)
    return [by_index(index, [parts[place ^ here] for here in range(count)]) for place in range(count)]


def head_plan(ctx_count, tile_heads):
    per = H // ctx_count
    wanted = [
        [per * c + i for i in range(per)] + [H + c, H + KVH + c] for c in range(ctx_count)
    ]
    sends = {}
    for dst in range(ctx_count):
        for head in wanted[dst]:
            sends.setdefault((head // tile_heads, dst), []).append(head)
    return wanted, sends


def exchange_heads(tile, axis, index):
    count = lax.axis_size(axis)
    tile_heads = tile.shape[1] // HD
    wanted, sends = head_plan(count, tile_heads)

    def head_of(block, k):
        return block[:, k * HD : (k + 1) * HD]

    arrived = {}
    for shift in range(count - 1, 0, -1):
        pairs = [(s, (s + shift) % count) for s in range(count) if (s, (s + shift) % count) in sends]
        if not pairs:
            continue
        width = max(len(sends[pair]) for pair in pairs)
        variants = []
        for s in range(count):
            heads = sends.get((s, (s + shift) % count), [])
            local = [head - s * tile_heads for head in heads]
            local = local + [0] * (width - len(local))
            variants.append(jnp.concatenate([head_of(tile, k) for k in local], axis=1))
        arrived[shift] = lax.ppermute(by_index(index, variants), axis, pairs)
    results = []
    for dst in range(count):
        pieces = []
        for head in wanted[dst]:
            src = head // tile_heads
            if src == dst:
                pieces.append(head_of(tile, head - src * tile_heads))
            else:
                block = arrived[(dst - src) % count]
                pieces.append(head_of(block, sends[(src, dst)].index(head)))
        results.append(jnp.concatenate(pieces, axis=1))
    return by_index(index, results)


def fast_shards(
    options,
    cache_keys,
    cache_values,
    attention_gain,
    expert_gain,
    input_weight,
    output_weight,
    router_weight,
    gate_weight,
    up_weight,
    down_weight,
    routing,
):
    own_rows = options[0]
    local_rows, model_width = own_rows.shape
    ctx_count = lax.axis_size("ctx")
    ctx_here = lax.axis_index("ctx")
    opt_here = lax.axis_index("opt")
    option_len = local_rows * ctx_count
    passage = cache_keys.shape[0] * ctx_count
    expert_count = router_weight.shape[1]
    top_count = routing.shape[2]
    group = H // KVH

    extra = jnp.zeros((local_rows, HD), jnp.bfloat16)
    extra = lax.dynamic_update_slice(extra, routing[0].astype(jnp.bfloat16), (0, 0))
    packed = jnp.concatenate([own_rows, extra], axis=1)
    packed = jnp.concatenate(gathered(packed, "ctx", ctx_here), axis=0)
    all_rows = packed[:, :model_width]
    chosen_ids = packed[:, model_width : model_width + top_count].astype(jnp.int32)

    def passage_head(who):
        return jnp.concatenate(
            [
                lax.dynamic_slice_in_dim(cache_keys, who * HD, HD, 1),
                lax.dynamic_slice_in_dim(cache_values, who * HD, HD, 1),
            ],
            axis=1,
        )

    passage_parts = [passage_head(ctx_here)]
    cache_seen, all_rows = lax.optimization_barrier(((cache_keys, cache_values), all_rows))
    cache_keys, cache_values = cache_seen
    for mask in range(ctx_count - 1, 0, -1):
        passage_parts.append(flip(passage_head(ctx_here ^ mask), "ctx", mask))

    normed = rms_scale(all_rows, attention_gain)
    product = jnp.dot(normed, input_weight, preferred_element_type=jnp.float32)
    first_head = ctx_here * (input_weight.shape[1] // HD)
    rotated = rotate(product, first_head, passage + jnp.arange(option_len)).astype(jnp.bfloat16)
    mine = exchange_heads(rotated, "ctx", ctx_here)

    queries = mine[:, : group * HD].reshape(option_len, group, HD)
    keys = jnp.concatenate([part[:, :HD] for part in passage_parts] + [mine[:, group * HD : (group + 1) * HD]], axis=0)
    values = jnp.concatenate([part[:, HD:] for part in passage_parts] + [mine[:, (group + 1) * HD :]], axis=0)
    scores = jnp.einsum("rgd,kd->grk", queries, keys, preferred_element_type=jnp.float32) * HD ** (-0.5)
    key_index = jnp.arange(keys.shape[0])
    visible = key_index[None, :] - passage <= jnp.arange(option_len)[:, None]
    scores = jnp.where(visible, scores, -jnp.inf)
    weights = jnp.exp(scores - jnp.max(scores, axis=-1, keepdims=True))
    totals = jnp.sum(weights, axis=-1)
    high = weights.astype(jnp.bfloat16)
    low = (weights - high.astype(jnp.float32)).astype(jnp.bfloat16)
    summed = jnp.einsum("grk,kd->grd", high, values, preferred_element_type=jnp.float32) + jnp.einsum(
        "grk,kd->grd", low, values, preferred_element_type=jnp.float32
    )
    attention = (summed / totals[..., None]).transpose(1, 0, 2).reshape(option_len, group * HD)
    attention = attention.astype(jnp.bfloat16)
    attention = jnp.concatenate(gathered(attention, "ctx", ctx_here), axis=1)
    out_width = output_weight.shape[1]
    columns = jnp.dot(attention, output_weight, preferred_element_type=jnp.float32).astype(jnp.bfloat16)
    own_columns = lax.dynamic_slice_in_dim(all_rows, ctx_here * out_width, out_width, 1)
    mixed_columns = (own_columns.astype(jnp.float32) + columns.astype(jnp.float32)).astype(jnp.bfloat16)
    mixed = jnp.concatenate(gathered(mixed_columns, "ctx", ctx_here), axis=1)

    expert_in = rms_scale(mixed, expert_gain)
    logits = jnp.dot(expert_in, router_weight, preferred_element_type=jnp.float32)
    matches = chosen_ids[:, :, None] == jnp.arange(expert_count)[None, None, :]
    picked = jnp.sum(jnp.where(matches, logits[:, None, :], 0.0), axis=-1)
    gate_share = jax.nn.softmax(picked, axis=-1)
    share_of = jnp.sum(jnp.where(matches, gate_share[:, :, None], 0.0), axis=1)
    named = jnp.any(matches, axis=1)
    earlier = jnp.arange(option_len)[None, :] < jnp.arange(option_len)[:, None]
    rank = jnp.sum(jnp.where(earlier[:, :, None] & named[None, :, :], 1, 0), axis=1)
    slots = MOST * ctx_count
    half = opt_here // 2
    own_expert = ctx_here * 2 + half
    other_expert = ctx_here * 2 + 1 - half

    def column(table, expert):
        here = jnp.arange(expert_count) == expert
        return jnp.sum(jnp.where(here[None, :], table, 0), axis=1)

    def choice(expert):
        taken = column(named.astype(jnp.int32), expert)
        place = column(rank, expert)
        hit = (place[None, :] == jnp.arange(slots)[:, None]) & (taken[None, :] == 1)
        share = jnp.sum(jnp.where(hit, column(share_of, expert)[None, :], 0.0), axis=1)
        return hit, share

    own_hit, own_share = choice(own_expert)
    other_hit, other_share = choice(other_expert)
    hits = jnp.concatenate([own_hit, other_hit], axis=0).astype(jnp.bfloat16)
    chosen_rows = jnp.dot(hits, expert_in, preferred_element_type=jnp.float32).astype(jnp.bfloat16)
    own_slots, other_slots = chosen_rows[:slots], chosen_rows[slots:]
    from_x = flip(other_slots, "opt", 2)
    core_own = flip(own_slots, "opt", 1)
    core_x = flip(from_x, "opt", 1)
    expert_rows = jnp.concatenate([own_slots, from_x, core_own, core_x], axis=0)

    hidden = expert_hidden(expert_rows, gate_weight, up_weight)
    partial_out = expert_down(hidden, down_weight, jnp.float32)
    from_core = flip(partial_out[2 * slots :].astype(jnp.bfloat16), "opt", 1)
    total = partial_out[: 2 * slots] + from_core.astype(jnp.float32)
    back = flip(total[slots:].astype(jnp.bfloat16), "opt", 2)
    shares = jnp.concatenate([own_share, other_share], axis=0)
    results = jnp.concatenate([total[:slots], back.astype(jnp.float32)], axis=0)
    weighted = (results * shares[:, None]).astype(jnp.bfloat16)
    spread = lax.dot_general(
        hits, weighted, (((0,), (0,)), ((), ())), preferred_element_type=jnp.float32
    )

    def rows_of(table, who):
        return lax.dynamic_slice_in_dim(table, who * local_rows, local_rows, 0)

    expert_sum = rows_of(spread, ctx_here)
    spread = spread.astype(jnp.bfloat16)
    for mask in range(ctx_count - 1, 0, -1):
        expert_sum = expert_sum + flip(rows_of(spread, ctx_here ^ mask), "ctx", mask).astype(jnp.float32)
    layer_out = (rows_of(mixed, ctx_here).astype(jnp.float32) + expert_sum).astype(jnp.bfloat16)
    return layer_out[None]


def takes_fast(mesh, options, input_weight, output_weight, router_weight, gate_weight):
    ctx_count, opt_count = mesh.shape["ctx"], mesh.shape["opt"]
    devices = ctx_count * opt_count
    return (
        ctx_count == KVH
        and opt_count == 4
        and router_weight.shape[1] == 2 * ctx_count
        and gate_weight.shape[1] == devices * (FF // 2)
        and input_weight.shape[1] % (ctx_count * HD) == 0
        and output_weight.shape[1] % (ctx_count * HD) == 0
    )


def solution(mesh):
    placed = (
        P(("parts", "opt"), "ctx", None),
        P(("parts", "ctx"), None),
        P(("parts", "ctx"), None),
        P(),
        P(),
        P(None, "ctx"),
        P(None, "ctx"),
        P(),
        P(None, ("ctx", "opt")),
        P(None, ("ctx", "opt")),
        P(("ctx", "opt"), None),
        P(("parts", "opt"), "ctx", None),
    )

    def layer(*args):
        fast = takes_fast(mesh, args[0], args[5], args[6], args[7], args[8])
        return jax.shard_map(
            fast_shards if fast else general_shards,
            mesh=mesh,
            in_specs=placed,
            out_specs=P(("parts", "opt"), "ctx", None),
            check_vma=False,
        )(*args)

    return layer
```

```python
import functools

import jax
import jax.numpy as jnp
from jax import lax
from jax.experimental import pallas as pl
from jax.experimental.pallas import tpu as pltpu
from jax.sharding import PartitionSpec as P

H = 24
KVH = 4
HD = 128
FF = 8192
MOST = 4


EPS = 1e-05
THETA = 1000000.0


def combined_all(x, axis, combine):
    everything = jax.tree.map(
        lambda part, kind: lax.all_gather(part.astype(kind), axis),
        x,
        (jnp.bfloat16, jnp.bfloat16, jnp.bfloat16),
    )

    def take(k):
        return jax.tree.map(lambda part, own: part[k].astype(own.dtype), everything, x)

    return lax.fori_loop(
        1, lax.axis_size(axis), lambda k, so_far: combine(so_far, take(k)), take(0)
    )


def rms_scale(row_data, gain_vector):
    floats = row_data.astype(jnp.float32)
    factor = lax.rsqrt(jnp.mean(floats * floats, axis=-1, keepdims=True) + EPS)
    return (floats * factor * gain_vector).astype(jnp.bfloat16)


def rotate(tile_data, first_head, positions):
    row_count, tile_width = tile_data.shape
    head_count = tile_width // HD
    half_dim = HD // 2
    split_view = tile_data.reshape(row_count, head_count, 2, half_dim)
    inverse = THETA ** (-2.0 * jnp.arange(half_dim, dtype=jnp.float32) / HD)
    angles = positions.astype(jnp.float32)[:, None] * inverse[None, :]
    cosine = jnp.cos(angles)[:, None, :]
    sine_part = jnp.sin(angles)[:, None, :]
    lower_half = split_view[:, :, 0]
    upper_half = split_view[:, :, 1]
    turned = jnp.stack(
        [
            lower_half * cosine - upper_half * sine_part,
            upper_half * cosine + lower_half * sine_part,
        ],
        axis=2,
    )
    rotated_head = first_head + jnp.arange(head_count) < H + KVH
    return jnp.where(rotated_head[None, :, None, None], turned, split_view).reshape(
        row_count, tile_width
    )


def softmax_parts(queries, key_rows, value_rows, key_start, cached):
    key_count = key_rows.shape[0]
    key_heads = key_rows.reshape(key_count, KVH, HD)
    value_heads = value_rows.reshape(key_count, KVH, HD).astype(jnp.float32)
    scores = jnp.einsum(
        "rhgd,khd->hgrk", queries, key_heads, preferred_element_type=jnp.float32
    ) * HD ** (-0.5)
    query_index = jnp.arange(queries.shape[0])
    key_index = jnp.arange(key_count)
    visible = (key_index[None, :] < cached) | (
        key_start + key_index[None, :] - cached <= query_index[:, None]
    )
    scores = jnp.where(visible, scores, -jnp.inf)
    maxima = jnp.max(scores, axis=-1)
    weights = jnp.exp(scores - maxima[..., None])
    totals = jnp.sum(weights, axis=-1)
    summed = jnp.einsum("hgrk,khd->hgrd", weights, value_heads, precision=lax.Precision.HIGHEST)
    return (maxima, totals, summed)


def join_parts(first, second):
    first_max, first_total, first_sum = first
    second_max, second_total, second_sum = second
    larger = jnp.maximum(first_max, second_max)
    first_scale = jnp.exp(first_max - larger)
    second_scale = jnp.exp(second_max - larger)
    return (
        larger,
        first_total * first_scale + second_total * second_scale,
        first_sum * first_scale[..., None] + second_sum * second_scale[..., None],
    )


def general_shards(
    options,
    cache_keys,
    cache_values,
    attention_gain,
    expert_gain,
    input_weight,
    output_weight,
    router_weight,
    gate_weight,
    up_weight,
    down_weight,
    routing,
):
    own_rows = options[0]
    ctx_count = lax.axis_size("ctx")
    ctx_here = lax.axis_index("ctx")
    local_rows = own_rows.shape[0]
    passage = cache_keys.shape[0] * ctx_count
    tile_columns = input_weight.shape[1]
    first_head = ctx_here * (tile_columns // HD)
    normed = rms_scale(own_rows, attention_gain)
    row_piece = lax.all_gather(normed, "ctx", axis=0, tiled=True)
    product = jnp.dot(row_piece, input_weight, preferred_element_type=jnp.float32)
    where_at = passage + jnp.int32(0) + jnp.arange(row_piece.shape[0])
    rotated_tile = rotate(product, first_head, where_at).astype(jnp.bfloat16)
    projected = lax.all_gather(rotated_tile, "ctx", axis=1, tiled=True)
    option_len = projected.shape[0]
    query_width = H * HD
    key_end = (H + KVH) * HD
    queries = projected[:, :query_width].reshape(option_len, KVH, H // KVH, HD)
    option_keys = projected[:, query_width:key_end]
    option_values = projected[:, key_end:]
    own_start = ctx_here * local_rows
    own_keys = lax.dynamic_slice_in_dim(option_keys, own_start, local_rows, 0)
    own_values = lax.dynamic_slice_in_dim(option_values, own_start, local_rows, 0)
    key_rows = jnp.concatenate([cache_keys, own_keys], axis=0)
    value_rows = jnp.concatenate([cache_values, own_values], axis=0)
    local_max, local_total, local_sum = softmax_parts(
        queries, key_rows, value_rows, own_start, cache_keys.shape[0]
    )
    maxima, totals, summed = combined_all((local_max, local_total, local_sum), "ctx", join_parts)
    attention = (
        (summed / totals[..., None])
        .transpose(2, 0, 1, 3)
        .reshape(option_len, query_width)
        .astype(jnp.bfloat16)
    )
    columns = jnp.dot(attention, output_weight, preferred_element_type=jnp.float32).astype(
        jnp.bfloat16
    )
    attention_out = lax.all_to_all(columns, "ctx", split_axis=0, concat_axis=1, tiled=True)
    mixed_in = (own_rows.astype(jnp.float32) + attention_out.astype(jnp.float32)).astype(
        jnp.bfloat16
    )
    expert_in = rms_scale(mixed_in, expert_gain)
    chosen_ids = routing[0]
    top_count = chosen_ids.shape[1]
    expert_count = router_weight.shape[1]
    logits = jnp.dot(expert_in, router_weight, preferred_element_type=jnp.float32)
    matches = chosen_ids[:, :, None] == jnp.arange(expert_count)[None, None, :]
    picked = jnp.sum(jnp.where(matches, logits[:, None, :], 0.0), axis=-1)
    gate_share = jax.nn.softmax(picked, axis=-1)
    ctx_width = expert_count * FF // ctx_count
    first_target = chosen_ids * FF // ctx_width
    last_target = ((chosen_ids + 1) * FF - 1) // ctx_width
    destination = jnp.arange(ctx_count)
    goes_to = (destination[None, None, :] >= first_target[:, :, None]) & (
        destination[None, None, :] <= last_target[:, :, None]
    )
    flat_goes = goes_to.reshape(local_rows * top_count, ctx_count).astype(jnp.int32)
    slot_index = jnp.cumsum(flat_goes, axis=0) - flat_goes
    slot_count = MOST * max(1, expert_count // ctx_count)
    slot_match = (flat_goes[:, :, None] == 1) & (
        slot_index[:, :, None] == jnp.arange(slot_count)[None, None, :]
    )
    slot_match = slot_match.reshape(local_rows, top_count, ctx_count * slot_count)
    token_slots = jnp.any(slot_match, axis=1).astype(jnp.bfloat16)
    model_width = expert_in.shape[1]
    outgoing = jnp.einsum(
        "rs,rd->sd", token_slots, expert_in, preferred_element_type=jnp.float32
    ).astype(jnp.bfloat16)
    outgoing = outgoing.reshape(ctx_count, slot_count, model_width)
    outgoing_ids = jnp.sum(jnp.where(slot_match, chosen_ids[:, :, None] + 1, 0), axis=(0, 1)) - 1
    outgoing_ids = outgoing_ids.reshape(ctx_count, slot_count)
    arrived, arrived_ids = (
        lax.all_to_all(outgoing, "ctx", split_axis=0, concat_axis=0, tiled=True),
        lax.all_to_all(outgoing_ids, "ctx", split_axis=0, concat_axis=0, tiled=True),
    )
    pooled, pooled_ids = (
        lax.all_gather(arrived, "opt", axis=0, tiled=True),
        lax.all_gather(arrived_ids, "opt", axis=0, tiled=True),
    )
    pooled = pooled.reshape(-1, model_width)
    pooled_ids = pooled_ids.reshape(-1)
    local_width = gate_weight.shape[1]
    opt_count = lax.axis_size("opt")
    column_start = (ctx_here * opt_count + lax.axis_index("opt")) * local_width
    column_expert = (column_start + jnp.arange(local_width)) // FF
    owned_mask = pooled_ids[:, None] == column_expert[None, :]
    gate_part = jnp.dot(pooled, gate_weight, preferred_element_type=jnp.float32)
    up_part = jnp.dot(pooled, up_weight, preferred_element_type=jnp.float32)
    hidden = jnp.where(owned_mask, jax.nn.silu(gate_part) * up_part, 0.0).astype(jnp.bfloat16)
    partial_out = jnp.dot(hidden, down_weight, preferred_element_type=jnp.float32)
    summed_back = lax.psum_scatter(
        partial_out.astype(jnp.bfloat16), "opt", scatter_dimension=0, tiled=True
    ).astype(jnp.float32)
    returned = lax.all_to_all(
        summed_back.reshape(ctx_count, slot_count, model_width).astype(jnp.bfloat16),
        "ctx",
        split_axis=0,
        concat_axis=0,
        tiled=True,
    ).astype(jnp.float32)
    weighting = jnp.sum(jnp.where(slot_match, gate_share[:, :, None], 0.0), axis=1)
    expert_sum = jnp.dot(
        weighting,
        returned.reshape(-1, model_width),
        precision=lax.Precision.HIGHEST,
        preferred_element_type=jnp.float32,
    )
    layer_out = (mixed_in.astype(jnp.float32) + expert_sum).astype(jnp.bfloat16)
    return layer_out[None]


def whole():
    return pl.BlockSpec(memory_space=pltpu.VMEM)


def anywhere():
    return pl.BlockSpec(memory_space=pl.ANY)


def kept(x):
    return pltpu.with_memory_space_constraint(x, pltpu.VMEM)


def scope(kind):
    return jax.named_scope(kind)


def flip(x, axis, mask):
    return lax.ppermute(x, axis, [(i, i ^ mask) for i in range(lax.axis_size(axis))])


def gathered(x, axis):
    masks = range(lax.axis_size(axis) - 1, 0, -1)
    return [x] + [flip(x, axis, mask) for mask in masks][::-1]


def aligned(index, size):
    return pl.ds(pl.multiple_of(index * size, size), size)


def cost(flops=0, bytes_accessed=0, transcendentals=0):
    return pl.CostEstimate(
        flops=flops, bytes_accessed=bytes_accessed, transcendentals=transcendentals
    )


def staged():
    return cost(flops=STAGE_FLOPS)


def params(limit):
    return pltpu.CompilerParams(vmem_limit_bytes=limit)


MIB = 1 << 20
STAGE_FLOPS = 8 * 10**9
EXPERT_MIB = 29


class Tiles:
    def __init__(self, source, buffers, sems):
        self.source, self.buffers, self.sems = source, buffers, sems
        self.slots, _, self.width = buffers.shape
        self.count = source.shape[1] // self.width

    def copy(self, i):
        slot = i % self.slots
        return pltpu.make_async_copy(
            self.source.at[:, pl.ds(i * self.width, self.width)],
            self.buffers.at[slot],
            self.sems.at[slot],
        )

    def start(self, i):
        if i < self.count:
            self.copy(i).start()

    def open(self):
        for i in range(self.slots):
            self.start(i)

    def ready(self, i):
        self.copy(i).wait()
        return self.buffers[i % self.slots]


def head_plan(ctx_count, tile_heads):
    per = H // ctx_count
    wanted = [
        [per * c + i for i in range(per)] + [H + c, H + KVH + c] for c in range(ctx_count)
    ]
    sends = {}
    for dst in range(ctx_count):
        for head in wanted[dst]:
            sends.setdefault((head // tile_heads, dst), []).append(head)
    pairs = {}
    for shift in range(1, ctx_count):
        found = [(s, (s + shift) % ctx_count) for s in range(ctx_count)]
        found = [pair for pair in found if pair in sends]
        if found:
            pairs[shift] = found
    return wanted, sends, pairs


def pack(cache_keys, cache_values, routing, ctx_count):
    passage_rows = cache_keys.shape[0]
    rows, top_count = routing.shape

    def kernel(keys_ref, values_ref, routing_ref, *out_refs):
        here = lax.axis_index("ctx")
        for mask, ref in enumerate(out_refs):
            ref[:passage_rows, :HD] = keys_ref[:, aligned(here ^ mask, HD)]
            ref[:passage_rows, HD:] = values_ref[:, aligned(here ^ mask, HD)]
            ref[passage_rows:, :] = jnp.zeros((rows, 2 * HD), jnp.bfloat16)
            ref[passage_rows:, :top_count] = routing_ref[...].astype(jnp.float32).astype(jnp.bfloat16)

    return pl.pallas_call(
        kernel,
        out_shape=[jax.ShapeDtypeStruct((passage_rows + rows, 2 * HD), jnp.bfloat16)] * ctx_count,
        in_specs=[whole()] * 3,
        out_specs=[whole()] * ctx_count,
        compiler_params=params(4 * MIB),
        cost_estimate=staged(),
        name="pack",
    )(cache_keys, cache_values, routing)


def project(parts, gain, weight, cosine, sine, plan):
    rows, width = parts[0].shape
    ctx_count = len(parts)
    total, columns = rows * ctx_count, weight.shape[1]
    heads = columns // HD
    _, sends, pairs = plan
    shifts = sorted(pairs)
    widths = [max(len(sends[pair]) for pair in pairs[shift]) * HD for shift in shifts]
    step = 4 * HD

    def kernel(*refs):
        part_refs = refs[:ctx_count]
        gain_ref, weight_ref, cosine_ref, sine_ref, tile_ref = refs[ctx_count : ctx_count + 5]
        payload_refs, (normed_ref, buffers, sems) = refs[ctx_count + 5 : -3], refs[-3:]
        here = lax.axis_index("ctx")
        tiles = Tiles(weight_ref, buffers, sems)
        tiles.open()
        for k in range(ctx_count):
            floats = part_refs[k][...].astype(jnp.float32)
            factor = lax.rsqrt(jnp.mean(floats * floats, axis=-1, keepdims=True) + EPS)
            normed_ref[aligned(here ^ k, rows), :] = floats * factor * gain_ref[...]
        normed = normed_ref[...].astype(jnp.bfloat16)
        for i in range(tiles.count):
            product = jnp.dot(normed, tiles.ready(i), preferred_element_type=jnp.float32)
            tiles.start(i + tiles.slots)
            for at in range(0, step, HD):
                head = (i * step + at) // HD
                plain = product[:, at : at + HD]
                turned = plain * cosine_ref[...] + pltpu.roll(plain, HD // 2, 1) * sine_ref[...]
                turned = jnp.where(here * heads + head < H + KVH, turned, plain)
                tile_ref[:, head * HD : (head + 1) * HD] = turned.astype(jnp.bfloat16)
        for s in range(ctx_count):

            @pl.when(here == s)
            def _():
                for shift, payload_ref in zip(shifts, payload_refs):
                    for place, head in enumerate(sends.get((s, (s + shift) % ctx_count), [])):
                        local = (head - s * heads) * HD
                        payload_ref[:, place * HD : (place + 1) * HD] = tile_ref[:, local : local + HD]

    out = pl.pallas_call(
        kernel,
        out_shape=[jax.ShapeDtypeStruct((total, n), jnp.bfloat16) for n in [columns] + widths],
        in_specs=[whole()] * (ctx_count + 1) + [anywhere()] + [whole()] * 2,
        out_specs=[whole()] * (1 + len(shifts)),
        scratch_shapes=[
            pltpu.VMEM((total, width), jnp.float32),
            pltpu.VMEM((2, width, step), jnp.bfloat16),
            pltpu.SemaphoreType.DMA((2,)),
        ],
        compiler_params=params(8 * MIB),
        cost_estimate=cost(bytes_accessed=2 * width * columns),
        name="project",
    )(*parts, gain[None], weight, cosine, sine)
    return out[0], dict(zip(shifts, out[1:]))


def attend(tile, arrived, passage_parts, plan, passage_rows):
    total = tile.shape[0]
    ctx_count = len(passage_parts)
    heads = tile.shape[1] // HD
    wanted, sends, _ = plan
    group = len(wanted[0]) - 2
    shifts = sorted(arrived)

    def kernel(*refs):
        tile_ref = refs[0]
        arrived_refs = dict(zip(shifts, refs[1 : 1 + len(shifts)]))
        passage_refs = refs[1 + len(shifts) : -2]
        out_ref, mine_ref = refs[-2:]
        here = lax.axis_index("ctx")
        for dst in range(ctx_count):

            @pl.when(here == dst)
            def _():
                for place, head in enumerate(wanted[dst]):
                    src = head // heads
                    if src == dst:
                        block, at = tile_ref, head - src * heads
                    else:
                        block = arrived_refs[(dst - src) % ctx_count]
                        at = sends[(src, dst)].index(head)
                    mine_ref[:, place * HD : (place + 1) * HD] = block[:, at * HD : (at + 1) * HD]

        def part(place):
            return mine_ref[:, place * HD : (place + 1) * HD]

        queries = jnp.concatenate([part(place) for place in range(group)], axis=0)
        keys = [ref[:passage_rows, :HD] for ref in passage_refs] + [part(group)]
        values = [ref[:passage_rows, HD:] for ref in passage_refs] + [part(group + 1)]
        scores = []
        for block in keys:
            scores.append(
                lax.dot_general(
                    queries, block, (((1,), (1,)), ((), ())), preferred_element_type=jnp.float32
                )
                * HD ** (-0.5)
            )
        token = lax.broadcasted_iota(jnp.int32, (total, total), 0)
        key = lax.broadcasted_iota(jnp.int32, (total, total), 1)
        bias = jnp.where(key <= token, 0.0, -jnp.inf)
        scores[-1] = scores[-1] + jnp.concatenate([bias] * group, axis=0)
        maxima = jnp.max(scores[0], axis=-1, keepdims=True)
        for block in scores[1:]:
            maxima = jnp.maximum(maxima, jnp.max(block, axis=-1, keepdims=True))
        sums, totals = 0.0, 0.0
        for block, value in zip(scores, values):
            weights = jnp.exp(block - maxima)
            totals = totals + jnp.sum(weights, axis=-1, keepdims=True)
            high = weights.astype(jnp.bfloat16)
            low = (weights - high.astype(jnp.float32)).astype(jnp.bfloat16)
            sums = sums + jnp.dot(high, value, preferred_element_type=jnp.float32)
            sums = sums + jnp.dot(low, value, preferred_element_type=jnp.float32)
        result = (sums / totals).astype(jnp.bfloat16)
        for place in range(group):
            out_ref[:, place * HD : (place + 1) * HD] = result[place * total : (place + 1) * total]

    return pl.pallas_call(
        kernel,
        out_shape=jax.ShapeDtypeStruct((total, group * HD), jnp.bfloat16),
        in_specs=[whole()] * (1 + len(shifts) + ctx_count),
        out_specs=whole(),
        scratch_shapes=[pltpu.VMEM((total, (group + 2) * HD), jnp.bfloat16)],
        compiler_params=params(6 * MIB),
        cost_estimate=staged(),
        name="attend",
    )(tile, *[arrived[shift] for shift in shifts], *passage_parts)


def out_project(attention, weight, parts):
    total, width = attention[0].shape
    rows = parts[0].shape[0]
    ctx_count = len(parts)
    columns = weight.shape[1]

    def kernel(*refs):
        attention_refs, weight_ref = refs[:ctx_count], refs[ctx_count]
        part_refs, (out_ref, raw_ref, near_ref, sems) = refs[ctx_count + 1 : -4], refs[-4:]
        here = lax.axis_index("ctx")

        def copy(k):
            return pltpu.make_async_copy(
                weight_ref.at[aligned(here ^ k, width), :], near_ref.at[k], sems.at[k]
            )

        for k in range(ctx_count):
            copy(k).start()
        for k in range(ctx_count):
            raw_ref[aligned(here ^ k, rows), :] = part_refs[k][:, aligned(here, columns)].astype(jnp.float32)
        product = jnp.zeros((total, columns), jnp.float32)
        for k in range(ctx_count):
            copy(k).wait()
            product = product + jnp.dot(
                attention_refs[k][...], near_ref[k], preferred_element_type=jnp.float32
            )
        product = product.astype(jnp.bfloat16).astype(jnp.float32)
        out_ref[...] = (raw_ref[...] + product).astype(jnp.bfloat16)

    return pl.pallas_call(
        kernel,
        out_shape=jax.ShapeDtypeStruct((total, columns), jnp.bfloat16),
        in_specs=[whole()] * ctx_count + [anywhere()] + [whole()] * ctx_count,
        out_specs=whole(),
        scratch_shapes=[
            pltpu.VMEM((total, columns), jnp.float32),
            pltpu.VMEM((ctx_count, width, columns), jnp.bfloat16),
            pltpu.SemaphoreType.DMA((ctx_count,)),
        ],
        compiler_params=params(7 * MIB),
        cost_estimate=cost(flops=STAGE_FLOPS, bytes_accessed=2 * width * ctx_count * columns),
        name="out_project",
    )(*attention, weight, *parts)


def route(mixed, gain, router, id_parts, slots):
    total, columns = mixed[0].shape
    ctx_count = len(mixed)
    rows = total // ctx_count
    width = columns * ctx_count
    expert_count = router.shape[0]

    def kernel(*refs):
        mixed_refs = refs[:ctx_count]
        gain_ref, router_ref = refs[ctx_count : ctx_count + 2]
        id_refs = refs[ctx_count + 2 : 2 * ctx_count + 2]
        own_ref, other_ref, rows_ref, place_ref, full_ref, ids_ref = refs[2 * ctx_count + 2 :]
        here = lax.axis_index("ctx")
        half = lax.axis_index("opt") // 2
        for k in range(ctx_count):
            full_ref[:, aligned(here ^ k, columns)] = mixed_refs[k][...].astype(jnp.float32)
            ids_ref[aligned(here ^ k, rows), :] = id_refs[k][:, :HD].astype(jnp.float32)
        floats = full_ref[...]
        factor = lax.rsqrt(jnp.mean(floats * floats, axis=-1, keepdims=True) + EPS)
        expert_in = (floats * factor * gain_ref[...]).astype(jnp.bfloat16)
        rows_ref[...] = full_ref[aligned(here, rows), :].astype(jnp.bfloat16)
        logits = lax.dot_general(
            expert_in, router_ref[...], (((1,), (1,)), ((), ())), preferred_element_type=jnp.float32
        )
        ids = ids_ref[...].astype(jnp.int32)
        lane = lax.broadcasted_iota(jnp.int32, (total, expert_count), 1)
        first, second = lane == ids[:, 0:1], lane == ids[:, 1:2]
        one = jnp.sum(jnp.where(first, logits, 0.0), axis=1, keepdims=True)
        two = jnp.sum(jnp.where(second, logits, 0.0), axis=1, keepdims=True)
        top = jnp.maximum(one, two)
        one, two = jnp.exp(one - top), jnp.exp(two - top)
        share = jnp.where(first, one / (one + two), 0.0) + jnp.where(second, two / (one + two), 0.0)
        named = jnp.where(first | second, 1.0, 0.0)
        row = lax.broadcasted_iota(jnp.int32, (total, total), 0)
        column = lax.broadcasted_iota(jnp.int32, (total, total), 1)
        earlier = jnp.where(column < row, 1.0, 0.0).astype(jnp.bfloat16)
        rank = jnp.dot(earlier, named.astype(jnp.bfloat16), preferred_element_type=jnp.float32)

        def of(expert, table):
            return jnp.sum(jnp.where(lane == expert, table, 0.0), axis=1, keepdims=True)

        slot = lax.broadcasted_iota(jnp.int32, (total, 2 * slots), 1)
        hits, weights = [], []
        for expert, low in ((here * 2 + half, 0), (here * 2 + 1 - half, slots)):
            place = of(expert, rank).astype(jnp.int32) + low
            inside = (slot >= low) & (slot < low + slots) & (of(expert, named) > 0.5)
            hit = jnp.where(inside & (place == slot), 1.0, 0.0)
            hits.append(hit)
            weights.append(hit * of(expert, share))
        hits = hits[0] + hits[1]
        place_ref[...] = weights[0] + weights[1]
        chosen = lax.dot_general(
            hits.astype(jnp.bfloat16),
            expert_in,
            (((0,), (0,)), ((), ())),
            preferred_element_type=jnp.float32,
        )
        own_ref[...] = chosen[:slots].astype(jnp.bfloat16)
        other_ref[...] = chosen[slots:].astype(jnp.bfloat16)

    return pl.pallas_call(
        kernel,
        out_shape=[
            jax.ShapeDtypeStruct((slots, width), jnp.bfloat16),
            jax.ShapeDtypeStruct((slots, width), jnp.bfloat16),
            jax.ShapeDtypeStruct((rows, width), jnp.bfloat16),
            jax.ShapeDtypeStruct((total, 2 * slots), jnp.float32),
        ],
        in_specs=[whole()] * (2 * ctx_count + 2),
        out_specs=[whole()] * 4,
        scratch_shapes=[
            pltpu.VMEM((total, width), jnp.float32),
            pltpu.VMEM((total, HD), jnp.float32),
        ],
        compiler_params=params(6 * MIB),
        cost_estimate=staged(),
        name="route",
    )(*mixed, gain[None], router, *id_parts)


def experts(blocks, gate, up, down, tile):
    slots, width = blocks[0].shape
    count = slots * len(blocks)
    units = gate.shape[1]
    up_slots, down_slots = 3, 4

    def kernel(*refs):
        block_refs, refs = refs[: len(blocks)], refs[len(blocks) :]
        gate_ref, up_ref, down_ref, own_ref, other_ref, send_ref = refs[:6]
        rows_ref, hidden_ref, ups_ref, downs_ref, up_sems, down_sems = refs[6:]
        ups = Tiles(up_ref, ups_ref, up_sems)
        downs = Tiles(down_ref, downs_ref, down_sems)
        ups.open()
        for k, ref in enumerate(block_refs):
            rows_ref[k * slots : (k + 1) * slots, :] = ref[...]
        early = 0
        for i in range(ups.count):
            at = slice(i * tile, (i + 1) * tile)
            a = jnp.dot(rows_ref[...], gate_ref[:, at], preferred_element_type=jnp.float32)
            b = jnp.dot(rows_ref[...], ups.ready(i), preferred_element_type=jnp.float32)
            ups.start(i + ups.slots)
            if (i % 2 == 1 or i + ups.slots >= ups.count) and early < downs.slots:
                downs.start(early)
                early += 1
            hidden_ref[:, at] = (a / (1.0 + jnp.exp(-a)) * b).astype(jnp.bfloat16)
        for i in range(early, downs.slots):
            downs.start(i)
        for i in range(downs.count):
            c = jnp.dot(hidden_ref[...], downs.ready(i), preferred_element_type=jnp.float32)
            downs.start(i + downs.slots)
            at = slice(i * tile, (i + 1) * tile)
            own_ref[:, at] = c[:slots]
            other_ref[:, at] = c[slots : 2 * slots]
            send_ref[:, at] = c[2 * slots :].astype(jnp.bfloat16)

    return pl.pallas_call(
        kernel,
        out_shape=[
            jax.ShapeDtypeStruct((slots, width), jnp.float32),
            jax.ShapeDtypeStruct((slots, width), jnp.float32),
            jax.ShapeDtypeStruct((2 * slots, width), jnp.bfloat16),
        ],
        in_specs=[whole()] * (len(blocks) + 1) + [anywhere()] * 2,
        out_specs=[whole()] * 3,
        scratch_shapes=[
            pltpu.VMEM((count, width), jnp.bfloat16),
            pltpu.VMEM((count, units), jnp.bfloat16),
            pltpu.VMEM((up_slots, width, tile), jnp.bfloat16),
            pltpu.VMEM((down_slots, units, tile), jnp.bfloat16),
            pltpu.SemaphoreType.DMA((up_slots,)),
            pltpu.SemaphoreType.DMA((down_slots,)),
        ],
        compiler_params=params(EXPERT_MIB * MIB),
        cost_estimate=cost(
            flops=6 * count * width * units, bytes_accessed=6 * width * units, transcendentals=count * units
        ),
        name="experts",
    )(*blocks, kept(gate), up, down)


def combine(own, from_core, back, place, ctx_count):
    slots, width = back.shape
    total = place.shape[0]
    rows = total // ctx_count

    def kernel(mine_ref, core_ref, back_ref, place_ref, own_ref, *refs):
        send_refs, spread_ref = refs[:-1], refs[-1]
        here = lax.axis_index("ctx")
        own = mine_ref[...] + core_ref[:slots, :].astype(jnp.float32)
        both = jnp.concatenate([own, back_ref[...].astype(jnp.float32)], axis=0)
        spread_ref[...] = jnp.dot(
            place_ref[...], both, precision=lax.Precision.HIGHEST, preferred_element_type=jnp.float32
        )
        own_ref[...] = spread_ref[aligned(here, rows), :]
        for k, ref in enumerate(send_refs):
            ref[...] = spread_ref[aligned(here ^ (k + 1), rows), :].astype(jnp.bfloat16)

    out = pl.pallas_call(
        kernel,
        out_shape=[jax.ShapeDtypeStruct((rows, width), jnp.float32)]
        + [jax.ShapeDtypeStruct((rows, width), jnp.bfloat16)] * (ctx_count - 1),
        in_specs=[whole()] * 4,
        out_specs=[whole()] * ctx_count,
        scratch_shapes=[pltpu.VMEM((total, width), jnp.float32)],
        compiler_params=params(6 * MIB),
        name="combine",
    )(own, from_core, back, place)
    return out[0], out[1:]


def fast_shards(
    options,
    cache_keys,
    cache_values,
    attention_gain,
    expert_gain,
    input_weight,
    output_weight,
    router_weight,
    gate_weight,
    up_weight,
    down_weight,
    routing,
):
    own_rows = options[0]
    local_rows, model_width = own_rows.shape
    ctx_count = lax.axis_size("ctx")
    ctx_here = lax.axis_index("ctx")
    option_len = local_rows * ctx_count
    passage_rows = cache_keys.shape[0]
    passage = passage_rows * ctx_count
    slots = MOST * ctx_count
    plan = head_plan(ctx_count, input_weight.shape[1] // HD)
    tile = 4 * HD

    with scope("rows"):
        parts = gathered(own_rows, "ctx")

    with scope("passage"):
        packed = pack(cache_keys, cache_values, routing[0], ctx_count)
        passage_parts = [packed[0]]
        passage_parts += [flip(packed[mask], "ctx", mask) for mask in range(1, ctx_count)]
    id_parts = [part[passage_rows:] for part in passage_parts]

    half_dim = HD // 2
    inverse = THETA ** (-2.0 * jnp.arange(half_dim, dtype=jnp.float32) / HD)
    positions = (passage + jnp.arange(option_len)).astype(jnp.float32)
    angles = positions[:, None] * inverse[None, :]
    cosine, sine = jnp.cos(angles), jnp.sin(angles)
    cosine = jnp.concatenate([cosine, cosine], axis=1)
    sine = jnp.concatenate([-sine, sine], axis=1)

    product, payloads = project(parts, attention_gain, input_weight, cosine, sine, plan)
    with scope("heads"):
        arrived = {shift: lax.ppermute(payloads[shift], "ctx", plan[2][shift]) for shift in payloads}
    attention = attend(product, arrived, passage_parts, plan, passage_rows)
    with scope("attention"):
        attention = gathered(attention, "ctx")
    mixed = out_project(attention, output_weight, parts)
    with scope("mixed"):
        mixed = gathered(mixed, "ctx")
    own_slots, other_slots, mixed_rows, place = route(
        mixed, expert_gain, router_weight.T, id_parts, slots
    )
    with scope("spread"):
        from_x = flip(other_slots, "opt", 2)
        core_own = flip(own_slots, "opt", 1)
    with scope("spread_core"):
        core_x = flip(from_x, "opt", 1)
    own, other, send = experts(
        [own_slots, from_x, core_own, core_x], gate_weight, up_weight, down_weight, tile
    )
    with scope("return"):
        from_core = flip(send, "opt", 1)
        other = (other + from_core[slots:].astype(jnp.float32)).astype(jnp.bfloat16)
        back = flip(other, "opt", 2)
    own_sum, sends = combine(own, from_core, back, place, ctx_count)
    with scope("finish"):
        total = mixed_rows.astype(jnp.float32) + own_sum
        for mask in range(ctx_count - 1, 0, -1):
            total = total + flip(sends[mask - 1], "ctx", mask).astype(jnp.float32)
    return total.astype(jnp.bfloat16)[None]


def takes_fast(mesh, options, input_weight, output_weight, router_weight, gate_weight):
    ctx_count, opt_count = mesh.shape["ctx"], mesh.shape["opt"]
    devices = ctx_count * opt_count
    return (
        ctx_count == KVH
        and opt_count == 4
        and router_weight.shape[1] == 2 * ctx_count
        and gate_weight.shape[1] == devices * (FF // 2)
        and input_weight.shape[1] % (ctx_count * HD) == 0
        and output_weight.shape[1] % (ctx_count * HD) == 0
    )


def solution(mesh):
    placed = (
        P(("parts", "opt"), "ctx", None),
        P(("parts", "ctx"), None),
        P(("parts", "ctx"), None),
        P(),
        P(),
        P(None, "ctx"),
        P(None, "ctx"),
        P(),
        P(None, ("ctx", "opt")),
        P(None, ("ctx", "opt")),
        P(("ctx", "opt"), None),
        P(("parts", "opt"), "ctx", None),
    )

    def layer(*args):
        fast = takes_fast(mesh, args[0], args[5], args[6], args[7], args[8])
        return jax.shard_map(
            fast_shards if fast else general_shards,
            mesh=mesh,
            in_specs=placed,
            out_specs=P(("parts", "opt"), "ctx", None),
            check_vma=False,
        )(*args)

    return layer
```

```python
import jax
import jax.numpy as jnp
from jax import lax
from jax.experimental import pallas as pl
from jax.experimental.pallas import tpu as pltpu
from jax.sharding import PartitionSpec as P


H = 24
KVH = 4
HD = 128
FF = 8192
MOST = 4


EPS = 1e-05
THETA = 1000000.0


def combined_all(x, axis, combine):
    everything = jax.tree.map(
        lambda part, kind: lax.all_gather(part.astype(kind), axis),
        x,
        (jnp.bfloat16, jnp.bfloat16, jnp.bfloat16),
    )

    def take(k):
        return jax.tree.map(lambda part, own: part[k].astype(own.dtype), everything, x)

    return lax.fori_loop(
        1, lax.axis_size(axis), lambda k, so_far: combine(so_far, take(k)), take(0)
    )


def rms_scale(row_data, gain_vector):
    floats = row_data.astype(jnp.float32)
    factor = lax.rsqrt(jnp.mean(floats * floats, axis=-1, keepdims=True) + EPS)
    return (floats * factor * gain_vector).astype(jnp.bfloat16)


def rotate(tile_data, first_head, positions):
    row_count, tile_width = tile_data.shape
    head_count = tile_width // HD
    half_dim = HD // 2
    split_view = tile_data.reshape(row_count, head_count, 2, half_dim)
    inverse = THETA ** (-2.0 * jnp.arange(half_dim, dtype=jnp.float32) / HD)
    angles = positions.astype(jnp.float32)[:, None] * inverse[None, :]
    cosine = jnp.cos(angles)[:, None, :]
    sine_part = jnp.sin(angles)[:, None, :]
    lower_half = split_view[:, :, 0]
    upper_half = split_view[:, :, 1]
    turned = jnp.stack(
        [
            lower_half * cosine - upper_half * sine_part,
            upper_half * cosine + lower_half * sine_part,
        ],
        axis=2,
    )
    rotated_head = first_head + jnp.arange(head_count) < H + KVH
    return jnp.where(rotated_head[None, :, None, None], turned, split_view).reshape(
        row_count, tile_width
    )


def softmax_parts(queries, key_rows, value_rows, key_start, cached):
    key_count = key_rows.shape[0]
    key_heads = key_rows.reshape(key_count, KVH, HD)
    value_heads = value_rows.reshape(key_count, KVH, HD).astype(jnp.float32)
    scores = jnp.einsum(
        "rhgd,khd->hgrk", queries, key_heads, preferred_element_type=jnp.float32
    ) * HD ** (-0.5)
    query_index = jnp.arange(queries.shape[0])
    key_index = jnp.arange(key_count)
    visible = (key_index[None, :] < cached) | (
        key_start + key_index[None, :] - cached <= query_index[:, None]
    )
    scores = jnp.where(visible, scores, -jnp.inf)
    maxima = jnp.max(scores, axis=-1)
    weights = jnp.exp(scores - maxima[..., None])
    totals = jnp.sum(weights, axis=-1)
    summed = jnp.einsum("hgrk,khd->hgrd", weights, value_heads, precision=lax.Precision.HIGHEST)
    return (maxima, totals, summed)


def join_parts(first, second):
    first_max, first_total, first_sum = first
    second_max, second_total, second_sum = second
    larger = jnp.maximum(first_max, second_max)
    first_scale = jnp.exp(first_max - larger)
    second_scale = jnp.exp(second_max - larger)
    return (
        larger,
        first_total * first_scale + second_total * second_scale,
        first_sum * first_scale[..., None] + second_sum * second_scale[..., None],
    )


def general_shards(
    options,
    cache_keys,
    cache_values,
    attention_gain,
    expert_gain,
    input_weight,
    output_weight,
    router_weight,
    gate_weight,
    up_weight,
    down_weight,
    routing,
):
    own_rows = options[0]
    ctx_count = lax.axis_size("ctx")
    ctx_here = lax.axis_index("ctx")
    local_rows = own_rows.shape[0]
    passage = cache_keys.shape[0] * ctx_count
    tile_columns = input_weight.shape[1]
    first_head = ctx_here * (tile_columns // HD)
    normed = rms_scale(own_rows, attention_gain)
    row_piece = lax.all_gather(normed, "ctx", axis=0, tiled=True)
    product = jnp.dot(row_piece, input_weight, preferred_element_type=jnp.float32)
    where_at = passage + jnp.int32(0) + jnp.arange(row_piece.shape[0])
    rotated_tile = rotate(product, first_head, where_at).astype(jnp.bfloat16)
    projected = lax.all_gather(rotated_tile, "ctx", axis=1, tiled=True)
    option_len = projected.shape[0]
    query_width = H * HD
    key_end = (H + KVH) * HD
    queries = projected[:, :query_width].reshape(option_len, KVH, H // KVH, HD)
    option_keys = projected[:, query_width:key_end]
    option_values = projected[:, key_end:]
    own_start = ctx_here * local_rows
    own_keys = lax.dynamic_slice_in_dim(option_keys, own_start, local_rows, 0)
    own_values = lax.dynamic_slice_in_dim(option_values, own_start, local_rows, 0)
    key_rows = jnp.concatenate([cache_keys, own_keys], axis=0)
    value_rows = jnp.concatenate([cache_values, own_values], axis=0)
    local_max, local_total, local_sum = softmax_parts(
        queries, key_rows, value_rows, own_start, cache_keys.shape[0]
    )
    _, totals, summed = combined_all((local_max, local_total, local_sum), "ctx", join_parts)
    attention = (
        (summed / totals[..., None])
        .transpose(2, 0, 1, 3)
        .reshape(option_len, query_width)
        .astype(jnp.bfloat16)
    )
    columns = jnp.dot(attention, output_weight, preferred_element_type=jnp.float32).astype(
        jnp.bfloat16
    )
    attention_out = lax.all_to_all(columns, "ctx", split_axis=0, concat_axis=1, tiled=True)
    mixed_in = (own_rows.astype(jnp.float32) + attention_out.astype(jnp.float32)).astype(
        jnp.bfloat16
    )
    expert_in = rms_scale(mixed_in, expert_gain)
    chosen_ids = routing[0]
    top_count = chosen_ids.shape[1]
    expert_count = router_weight.shape[1]
    logits = jnp.dot(expert_in, router_weight, preferred_element_type=jnp.float32)
    matches = chosen_ids[:, :, None] == jnp.arange(expert_count)[None, None, :]
    picked = jnp.sum(jnp.where(matches, logits[:, None, :], 0.0), axis=-1)
    gate_share = jax.nn.softmax(picked, axis=-1)
    ctx_width = expert_count * FF // ctx_count
    first_target = chosen_ids * FF // ctx_width
    last_target = ((chosen_ids + 1) * FF - 1) // ctx_width
    destination = jnp.arange(ctx_count)
    goes_to = (destination[None, None, :] >= first_target[:, :, None]) & (
        destination[None, None, :] <= last_target[:, :, None]
    )
    flat_goes = goes_to.reshape(local_rows * top_count, ctx_count).astype(jnp.int32)
    slot_index = jnp.cumsum(flat_goes, axis=0) - flat_goes
    slot_count = MOST * max(1, expert_count // ctx_count)
    slot_match = (flat_goes[:, :, None] == 1) & (
        slot_index[:, :, None] == jnp.arange(slot_count)[None, None, :]
    )
    slot_match = slot_match.reshape(local_rows, top_count, ctx_count * slot_count)
    token_slots = jnp.any(slot_match, axis=1).astype(jnp.bfloat16)
    model_width = expert_in.shape[1]
    outgoing = jnp.einsum(
        "rs,rd->sd", token_slots, expert_in, preferred_element_type=jnp.float32
    ).astype(jnp.bfloat16)
    outgoing = outgoing.reshape(ctx_count, slot_count, model_width)
    outgoing_ids = jnp.sum(jnp.where(slot_match, chosen_ids[:, :, None] + 1, 0), axis=(0, 1)) - 1
    outgoing_ids = outgoing_ids.reshape(ctx_count, slot_count)
    arrived, arrived_ids = (
        lax.all_to_all(outgoing, "ctx", split_axis=0, concat_axis=0, tiled=True),
        lax.all_to_all(outgoing_ids, "ctx", split_axis=0, concat_axis=0, tiled=True),
    )
    pooled, pooled_ids = (
        lax.all_gather(arrived, "opt", axis=0, tiled=True),
        lax.all_gather(arrived_ids, "opt", axis=0, tiled=True),
    )
    pooled = pooled.reshape(-1, model_width)
    pooled_ids = pooled_ids.reshape(-1)
    local_width = gate_weight.shape[1]
    opt_count = lax.axis_size("opt")
    column_start = (ctx_here * opt_count + lax.axis_index("opt")) * local_width
    column_expert = (column_start + jnp.arange(local_width)) // FF
    owned_mask = pooled_ids[:, None] == column_expert[None, :]
    gate_part = jnp.dot(pooled, gate_weight, preferred_element_type=jnp.float32)
    up_part = jnp.dot(pooled, up_weight, preferred_element_type=jnp.float32)
    hidden = jnp.where(owned_mask, jax.nn.silu(gate_part) * up_part, 0.0).astype(jnp.bfloat16)
    partial_out = jnp.dot(hidden, down_weight, preferred_element_type=jnp.float32)
    summed_back = lax.psum_scatter(
        partial_out.astype(jnp.bfloat16), "opt", scatter_dimension=0, tiled=True
    ).astype(jnp.float32)
    returned = lax.all_to_all(
        summed_back.reshape(ctx_count, slot_count, model_width).astype(jnp.bfloat16),
        "ctx",
        split_axis=0,
        concat_axis=0,
        tiled=True,
    ).astype(jnp.float32)
    weighting = jnp.sum(jnp.where(slot_match, gate_share[:, :, None], 0.0), axis=1)
    expert_sum = jnp.dot(
        weighting,
        returned.reshape(-1, model_width),
        precision=lax.Precision.HIGHEST,
        preferred_element_type=jnp.float32,
    )
    layer_out = (mixed_in.astype(jnp.float32) + expert_sum).astype(jnp.bfloat16)
    return layer_out[None]


def whole():
    return pl.BlockSpec(memory_space=pltpu.VMEM)


def anywhere():
    return pl.BlockSpec(memory_space=pl.ANY)


def kept(x):
    return pltpu.with_memory_space_constraint(x, pltpu.VMEM)


def flip(x, axis, mask):
    return lax.ppermute(x, axis, [(i, i ^ mask) for i in range(lax.axis_size(axis))])


def gathered(x, axis):
    masks = range(lax.axis_size(axis) - 1, 0, -1)
    return [x] + [flip(x, axis, mask) for mask in masks][::-1]


def aligned(index, size):
    return pl.ds(pl.multiple_of(index * size, size), size)


def cost(flops=0, bytes_accessed=0, transcendentals=0):
    return pl.CostEstimate(
        flops=flops, bytes_accessed=bytes_accessed, transcendentals=transcendentals
    )


def staged():
    return cost(flops=STAGE_FLOPS)


def params(limit):
    return pltpu.CompilerParams(vmem_limit_bytes=limit)


MIB = 1 << 20
STAGE_FLOPS = 8 * 10**9
HEADS_ORDER = (1, 2, 3)
EXPERT_MIB = 11


class Tiles:
    def __init__(self, source, buffers, sems):
        self.source, self.buffers, self.sems = source, buffers, sems
        self.slots, _, self.width = buffers.shape
        self.count = source.shape[1] // self.width

    def copy(self, i):
        slot = i % self.slots
        return pltpu.make_async_copy(
            self.source.at[:, pl.ds(i * self.width, self.width)],
            self.buffers.at[slot],
            self.sems.at[slot],
        )

    def start(self, i):
        if i < self.count:
            self.copy(i).start()

    def open(self):
        for i in range(self.slots):
            self.start(i)

    def ready(self, i):
        self.copy(i).wait()
        return self.buffers[i % self.slots]


def head_plan(ctx_count, tile_heads):
    per = H // ctx_count
    wanted = [
        [per * c + i for i in range(per)] + [H + c, H + KVH + c] for c in range(ctx_count)
    ]
    sends = {}
    for dst in range(ctx_count):
        for head in wanted[dst]:
            sends.setdefault((head // tile_heads, dst), []).append(head)
    pairs = {}
    for shift in range(1, ctx_count):
        found = [(s, (s + shift) % ctx_count) for s in range(ctx_count)]
        found = [pair for pair in found if pair in sends]
        if found:
            pairs[shift] = found
    return wanted, sends, pairs


def tables(cosine, sine):
    def kernel(cosine_ref, sine_ref, cosine_out, sine_out):
        cosine_out[...] = cosine_ref[...]
        sine_out[...] = sine_ref[...]

    return pl.pallas_call(
        kernel,
        out_shape=[jax.ShapeDtypeStruct(cosine.shape, cosine.dtype)] * 2,
        in_specs=[whole()] * 2,
        out_specs=[whole()] * 2,
        compiler_params=params(2 * MIB),
        cost_estimate=staged(),
        name="tables",
    )(cosine, sine)


def pack(cache_keys, cache_values, routing, after):
    passage_rows = cache_keys.shape[0]
    top_count, rows = routing.shape
    half = passage_rows // 2

    def kernel(keys_ref, values_ref, routing_ref, after_ref, *refs):
        out_refs, ids_ref = refs[:-1], refs[-1]
        here = lax.axis_index("ctx")
        core = lax.axis_index("opt") % 2
        row = lax.broadcasted_iota(jnp.int32, (rows, rows), 0)
        column = lax.broadcasted_iota(jnp.int32, (rows, rows), 1)
        lane = lax.broadcasted_iota(jnp.int32, (rows, HD), 1)
        numbers = jnp.zeros((rows, HD), jnp.float32)
        for k in range(top_count):
            spread = jnp.where(row == column, routing_ref[k : k + 1, :].astype(jnp.float32), 0.0)
            numbers = numbers + jnp.where(lane == k, jnp.sum(spread, axis=1, keepdims=True), 0.0)
        for ref, who in zip(out_refs, (here, here ^ (1 + core), here ^ 3)):
            count = ref.shape[0]
            start = 0 if count == passage_rows else pl.multiple_of(core * half, half)
            for side, source in enumerate((keys_ref, values_ref)):
                ref[:, side * HD : (side + 1) * HD] = source[pl.ds(start, count), aligned(who, HD)]
        ids_ref[...] = numbers.astype(jnp.bfloat16)

    return pl.pallas_call(
        kernel,
        out_shape=[
            jax.ShapeDtypeStruct((count, 2 * HD), jnp.bfloat16)
            for count in (passage_rows, passage_rows, half)
        ]
        + [jax.ShapeDtypeStruct((rows, HD), jnp.bfloat16)],
        in_specs=[whole()] * 3 + [anywhere()],
        out_specs=[whole()] * 4,
        compiler_params=params(4 * MIB),
        cost_estimate=staged(),
        name="pack",
    )(cache_keys, cache_values, routing, after)


def project(parts, gain, weight, cosine, sine, plan):
    rows, width = parts[0].shape
    ctx_count = len(parts)
    total, columns = rows * ctx_count, weight.shape[1]
    heads = columns // HD
    _, sends, pairs = plan
    shifts = sorted(pairs)
    widths = [max(len(sends[pair]) for pair in pairs[shift]) * HD for shift in shifts]
    step = 4 * HD

    def kernel(*refs):
        part_refs = refs[:ctx_count]
        gain_ref, weight_ref, cosine_ref, sine_ref, tile_ref = refs[ctx_count : ctx_count + 5]
        payload_refs, normed_ref = refs[ctx_count + 5 : -1], refs[-1]
        here = lax.axis_index("ctx")
        for k in range(ctx_count):
            floats = part_refs[k][...].astype(jnp.float32)
            factor = lax.rsqrt(jnp.mean(floats * floats, axis=-1, keepdims=True) + EPS)
            normed_ref[aligned(here ^ k, rows), :] = floats * factor * gain_ref[...]
        normed = normed_ref[...].astype(jnp.bfloat16)
        for i in range(columns // step):
            product = jnp.dot(
                normed, weight_ref[:, i * step : (i + 1) * step], preferred_element_type=jnp.float32
            )
            for at in range(0, step, HD):
                head = (i * step + at) // HD
                plain = product[:, at : at + HD]
                turned = plain * cosine_ref[...] + pltpu.roll(plain, HD // 2, 1) * sine_ref[...]
                turned = jnp.where(here * heads + head < H + KVH, turned, plain)
                tile_ref[:, head * HD : (head + 1) * HD] = turned.astype(jnp.bfloat16)
        for s in range(ctx_count):

            @pl.when(here == s)
            def _():
                for shift, payload_ref in zip(shifts, payload_refs):
                    for place, head in enumerate(sends.get((s, (s + shift) % ctx_count), [])):
                        local = (head - s * heads) * HD
                        payload_ref[:, place * HD : (place + 1) * HD] = tile_ref[:, local : local + HD]

    out = pl.pallas_call(
        kernel,
        out_shape=[jax.ShapeDtypeStruct((total, n), jnp.bfloat16) for n in [columns] + widths],
        in_specs=[whole()] * (ctx_count + 4),
        out_specs=[whole()] * (1 + len(shifts)),
        scratch_shapes=[pltpu.VMEM((total, width), jnp.float32)],
        compiler_params=params(4 * MIB),
        cost_estimate=cost(bytes_accessed=2 * width * columns),
        name="project",
    )(*parts, gain[None], kept(weight), cosine, sine)
    return out[0], dict(zip(shifts, out[1:]))


def attend(tile, arrived, passage_parts, ids, plan):
    total, rows = tile.shape[0], ids.shape[0]
    ctx_count = lax.axis_size("ctx")
    heads = tile.shape[1] // HD
    wanted, sends, _ = plan
    group = len(wanted[0]) - 2
    shifts = sorted(arrived)

    def kernel(*refs):
        tile_ref = refs[0]
        arrived_refs = dict(zip(shifts, refs[1 : 1 + len(shifts)]))
        passage_refs = refs[1 + len(shifts) : -3]
        numbers_ref, out_ref, mine_ref = refs[-3:]
        here = lax.axis_index("ctx")
        for dst in range(ctx_count):

            @pl.when(here == dst)
            def _():
                for place, head in enumerate(wanted[dst]):
                    src = head // heads
                    if src == dst:
                        block, at = tile_ref, head - src * heads
                    else:
                        block = arrived_refs[(dst - src) % ctx_count]
                        at = sends[(src, dst)].index(head)
                    mine_ref[:, place * HD : (place + 1) * HD] = block[:, at * HD : (at + 1) * HD]

        def part(place):
            return mine_ref[:, place * HD : (place + 1) * HD]

        queries = jnp.concatenate([part(place) for place in range(group)], axis=0)
        keys = [ref[:, :HD] for ref in passage_refs] + [part(group)]
        values = [ref[:, HD:] for ref in passage_refs] + [part(group + 1)]
        scores = []
        for block in keys:
            scores.append(
                lax.dot_general(
                    queries, block, (((1,), (1,)), ((), ())), preferred_element_type=jnp.float32
                )
                * HD ** (-0.5)
            )
        token = lax.broadcasted_iota(jnp.int32, (total, total), 0)
        key = lax.broadcasted_iota(jnp.int32, (total, total), 1)
        bias = jnp.where(key <= token, 0.0, -jnp.inf)
        scores[-1] = scores[-1] + jnp.concatenate([bias] * group, axis=0)
        maxima = jnp.max(scores[0], axis=-1, keepdims=True)
        for block in scores[1:]:
            maxima = jnp.maximum(maxima, jnp.max(block, axis=-1, keepdims=True))
        sums, totals = 0.0, 0.0
        for block, value in zip(scores, values):
            weights = jnp.exp(block - maxima)
            totals = totals + jnp.sum(weights, axis=-1, keepdims=True)
            high = weights.astype(jnp.bfloat16)
            low = (weights - high.astype(jnp.float32)).astype(jnp.bfloat16)
            sums = sums + jnp.dot(high, value, preferred_element_type=jnp.float32)
            sums = sums + jnp.dot(low, value, preferred_element_type=jnp.float32)
        result = (sums / totals).astype(jnp.bfloat16)
        for place in range(group):
            out_ref[:total, place * HD : (place + 1) * HD] = result[place * total : (place + 1) * total]
        out_ref[total:, :] = jnp.zeros((rows, group * HD), jnp.bfloat16)
        out_ref[total:, :HD] = numbers_ref[...]

    return pl.pallas_call(
        kernel,
        out_shape=jax.ShapeDtypeStruct((total + rows, group * HD), jnp.bfloat16),
        in_specs=[whole()] * (2 + len(shifts) + len(passage_parts)),
        out_specs=whole(),
        scratch_shapes=[pltpu.VMEM((total, (group + 2) * HD), jnp.bfloat16)],
        compiler_params=params(6 * MIB),
        cost_estimate=staged(),
        name="attend",
    )(tile, *[arrived[shift] for shift in shifts], *passage_parts, ids)


def out_project(attention, weight, parts):
    width = attention[0].shape[1]
    rows = parts[0].shape[0]
    ctx_count = len(parts)
    total = rows * ctx_count
    columns = weight.shape[1]

    def kernel(*refs):
        attention_refs, weight_ref = refs[:ctx_count], refs[ctx_count]
        part_refs, (out_ref, raw_ref) = refs[ctx_count + 1 : -2], refs[-2:]
        here = lax.axis_index("ctx")
        for k in range(ctx_count):
            raw_ref[aligned(here ^ k, rows), :] = part_refs[k][:, aligned(here, columns)].astype(jnp.float32)
        product = jnp.zeros((total, columns), jnp.float32)
        for k in range(ctx_count):
            product = product + jnp.dot(
                attention_refs[k][:total, :],
                weight_ref[aligned(here ^ k, width), :],
                preferred_element_type=jnp.float32,
            )
        product = product.astype(jnp.bfloat16).astype(jnp.float32)
        out_ref[...] = (raw_ref[...] + product).astype(jnp.bfloat16)

    return pl.pallas_call(
        kernel,
        out_shape=jax.ShapeDtypeStruct((total, columns), jnp.bfloat16),
        in_specs=[whole()] * (2 * ctx_count + 1),
        out_specs=whole(),
        scratch_shapes=[pltpu.VMEM((total, columns), jnp.float32)],
        compiler_params=params(4 * MIB),
        cost_estimate=cost(flops=STAGE_FLOPS, bytes_accessed=2 * width * ctx_count * columns),
        name="out_project",
    )(*attention, kept(weight), *parts)


def route(mixed, gain, router, id_parts, slots):
    total, columns = mixed[0].shape
    ctx_count = len(mixed)
    rows = total // ctx_count
    width = columns * ctx_count
    expert_count = router.shape[0]

    def kernel(*refs):
        mixed_refs = refs[:ctx_count]
        gain_ref, router_ref = refs[ctx_count : ctx_count + 2]
        id_refs = refs[ctx_count + 2 : 2 * ctx_count + 2]
        own_ref, other_ref, rows_ref, place_ref, full_ref, ids_ref = refs[2 * ctx_count + 2 :]
        here = lax.axis_index("ctx")
        half = lax.axis_index("opt") // 2
        for k in range(ctx_count):
            full_ref[:, aligned(here ^ k, columns)] = mixed_refs[k][...].astype(jnp.float32)
            ids_ref[aligned(here ^ k, rows), :] = id_refs[k][total:, :HD].astype(jnp.float32)
        floats = full_ref[...]
        factor = lax.rsqrt(jnp.mean(floats * floats, axis=-1, keepdims=True) + EPS)
        expert_in = (floats * factor * gain_ref[...]).astype(jnp.bfloat16)
        rows_ref[...] = full_ref[aligned(here, rows), :].astype(jnp.bfloat16)
        logits = lax.dot_general(
            expert_in, router_ref[...], (((1,), (1,)), ((), ())), preferred_element_type=jnp.float32
        )
        ids = ids_ref[...].astype(jnp.int32)
        lane = lax.broadcasted_iota(jnp.int32, (total, expert_count), 1)
        first, second = lane == ids[:, 0:1], lane == ids[:, 1:2]
        one = jnp.sum(jnp.where(first, logits, 0.0), axis=1, keepdims=True)
        two = jnp.sum(jnp.where(second, logits, 0.0), axis=1, keepdims=True)
        top = jnp.maximum(one, two)
        one, two = jnp.exp(one - top), jnp.exp(two - top)
        share = jnp.where(first, one / (one + two), 0.0) + jnp.where(second, two / (one + two), 0.0)
        named = jnp.where(first | second, 1.0, 0.0)
        row = lax.broadcasted_iota(jnp.int32, (total, total), 0)
        column = lax.broadcasted_iota(jnp.int32, (total, total), 1)
        earlier = jnp.where(column < row, 1.0, 0.0).astype(jnp.bfloat16)
        rank = jnp.dot(earlier, named.astype(jnp.bfloat16), preferred_element_type=jnp.float32)

        def of(expert, table):
            return jnp.sum(jnp.where(lane == expert, table, 0.0), axis=1, keepdims=True)

        slot = lax.broadcasted_iota(jnp.int32, (total, 2 * slots), 1)
        hits, weights = [], []
        for expert, low in ((here * 2 + half, 0), (here * 2 + 1 - half, slots)):
            place = of(expert, rank).astype(jnp.int32) + low
            inside = (slot >= low) & (slot < low + slots) & (of(expert, named) > 0.5)
            hit = jnp.where(inside & (place == slot), 1.0, 0.0)
            hits.append(hit)
            weights.append(hit * of(expert, share))
        hits = hits[0] + hits[1]
        place_ref[...] = weights[0] + weights[1]
        chosen = lax.dot_general(
            hits.astype(jnp.bfloat16),
            expert_in,
            (((0,), (0,)), ((), ())),
            preferred_element_type=jnp.float32,
        )
        own_ref[...] = chosen[:slots].astype(jnp.bfloat16)
        other_ref[...] = chosen[slots:].astype(jnp.bfloat16)

    return pl.pallas_call(
        kernel,
        out_shape=[
            jax.ShapeDtypeStruct((slots, width), jnp.bfloat16),
            jax.ShapeDtypeStruct((slots, width), jnp.bfloat16),
            jax.ShapeDtypeStruct((rows, width), jnp.bfloat16),
            jax.ShapeDtypeStruct((total, 2 * slots), jnp.float32),
        ],
        in_specs=[whole()] * (2 * ctx_count + 2),
        out_specs=[whole()] * 4,
        scratch_shapes=[
            pltpu.VMEM((total, width), jnp.float32),
            pltpu.VMEM((total, HD), jnp.float32),
        ],
        compiler_params=params(6 * MIB),
        cost_estimate=staged(),
        name="route",
    )(*mixed, gain[None], router, *id_parts)


def experts(blocks, gate, up, down, tile):
    slots, width = blocks[0].shape
    count = slots * len(blocks)
    units = gate.shape[1]
    up_slots = 2
    tall = max(count, 128)

    def kernel(*refs):
        block_refs, refs = refs[: len(blocks)], refs[len(blocks) :]
        gate_ref, up_ref, down_ref, own_ref, other_ref, send_ref = refs[:6]
        rows_ref, hidden_ref, total_ref, ups_ref, up_sems = refs[6:]
        ups = Tiles(up_ref, ups_ref, up_sems)
        ups.open()
        for k in range(tall // slots):
            rows_ref[k * slots : (k + 1) * slots, :] = block_refs[k % len(blocks)][...]

        def add_down(i):
            at = slice(i * tile, (i + 1) * tile)
            hidden = hidden_ref[i % 2]
            for start in range(0, width, 2 * tile):
                cut = slice(start, start + 2 * tile)
                c = jnp.dot(hidden, down_ref[at, cut], preferred_element_type=jnp.float32)[:count]
                total_ref[:, cut] = c if i == 0 else total_ref[:, cut] + c

        for i in range(ups.count):
            at = slice(i * tile, (i + 1) * tile)
            a = jnp.dot(rows_ref[...], gate_ref[:, at], preferred_element_type=jnp.float32)[:count]
            b = jnp.dot(rows_ref[...], ups.ready(i), preferred_element_type=jnp.float32)[:count]
            ups.start(i + ups.slots)
            if i > 0:
                add_down(i - 1)
            hidden = (a / (1.0 + jnp.exp(-a)) * b).astype(jnp.bfloat16)
            for k in range(tall // count):
                hidden_ref[i % 2, k * count : (k + 1) * count, :] = hidden
        add_down(ups.count - 1)
        own_ref[...] = total_ref[:slots, :]
        other_ref[...] = total_ref[slots : 2 * slots, :]
        send_ref[...] = total_ref[2 * slots :, :].astype(jnp.bfloat16)

    return pl.pallas_call(
        kernel,
        out_shape=[
            pltpu.VMEM((slots, width), jnp.float32),
            pltpu.VMEM((slots, width), jnp.float32),
            pltpu.VMEM((2 * slots, width), jnp.bfloat16),
        ],
        in_specs=[whole()] * (len(blocks) + 1) + [anywhere(), whole()],
        out_specs=[whole()] * 3,
        scratch_shapes=[
            pltpu.VMEM((tall, width), jnp.bfloat16),
            pltpu.VMEM((2, tall, tile), jnp.bfloat16),
            pltpu.VMEM((count, width), jnp.float32),
            pltpu.VMEM((up_slots, width, tile), jnp.bfloat16),
            pltpu.SemaphoreType.DMA((up_slots,)),
        ],
        compiler_params=params(EXPERT_MIB * MIB),
        cost_estimate=cost(
            flops=6 * count * width * units, bytes_accessed=6 * width * units, transcendentals=count * units
        ),
        name="experts",
    )(*[kept(block) for block in blocks], kept(gate), up, kept(down))


def merge(other, from_core):
    slots, width = other.shape

    def kernel(mine_ref, core_ref, out_ref):
        out_ref[...] = (mine_ref[...] + core_ref[slots:, :].astype(jnp.float32)).astype(jnp.bfloat16)

    return pl.pallas_call(
        kernel,
        out_shape=jax.ShapeDtypeStruct((slots, width), jnp.bfloat16),
        in_specs=[whole()] * 2,
        out_specs=whole(),
        compiler_params=params(4 * MIB),
        name="merge",
    )(kept(other), from_core)


def combine(own, from_core, back, place, ctx_count):
    slots, width = back.shape
    total = place.shape[0]
    rows = total // ctx_count

    def kernel(mine_ref, core_ref, back_ref, place_ref, own_ref, *refs):
        send_refs, spread_ref = refs[:-1], refs[-1]
        here = lax.axis_index("ctx")
        own = mine_ref[...] + core_ref[:slots, :].astype(jnp.float32)
        both = jnp.concatenate([own, back_ref[...].astype(jnp.float32)], axis=0)
        spread_ref[...] = jnp.dot(
            place_ref[...], both, precision=lax.Precision.HIGHEST, preferred_element_type=jnp.float32
        )
        own_ref[...] = spread_ref[aligned(here, rows), :]
        for k, ref in enumerate(send_refs):
            ref[...] = spread_ref[aligned(here ^ (k + 1), rows), :].astype(jnp.bfloat16)

    out = pl.pallas_call(
        kernel,
        out_shape=[jax.ShapeDtypeStruct((rows, width), jnp.float32)]
        + [jax.ShapeDtypeStruct((rows, width), jnp.bfloat16)] * (ctx_count - 1),
        in_specs=[whole()] * 4,
        out_specs=[whole()] * ctx_count,
        scratch_shapes=[pltpu.VMEM((total, width), jnp.float32)],
        compiler_params=params(6 * MIB),
        name="combine",
    )(kept(own), from_core, back, place)
    return out[0], out[1:]


def fast_shards(*args):
    return fast_layer(*args)


def fast_layer(
    options,
    cache_keys,
    cache_values,
    attention_gain,
    expert_gain,
    input_weight,
    output_weight,
    router_weight,
    gate_weight,
    up_weight,
    down_weight,
    routing,
):
    own_rows = options[0]
    local_rows, _ = own_rows.shape
    ctx_count = lax.axis_size("ctx")
    option_len = local_rows * ctx_count
    passage_rows = cache_keys.shape[0]
    passage = passage_rows * ctx_count
    slots = MOST * ctx_count
    plan = head_plan(ctx_count, input_weight.shape[1] // HD)
    tile = 4 * HD

    parts = gathered(own_rows, "ctx")

    half_dim = HD // 2
    inverse = THETA ** (-2.0 * jnp.arange(half_dim, dtype=jnp.float32) / HD)
    positions = (passage + jnp.arange(option_len)).astype(jnp.float32)
    angles = positions[:, None] * inverse[None, :]
    cosine, sine = jnp.cos(angles), jnp.sin(angles)
    cosine = jnp.concatenate([cosine, cosine], axis=1)
    sine = jnp.concatenate([-sine, sine], axis=1)
    cosine, sine = tables(cosine, sine)

    packed = pack(cache_keys, cache_values, routing[0].T, cosine)
    opt_count = lax.axis_size("opt")
    places = [(c, o) for c in range(ctx_count) for o in range(opt_count)]
    to_one = [(c * opt_count + o, (c ^ (1 + o % 2)) * opt_count + o) for c, o in places]
    one = lax.ppermute(packed[1], ("ctx", "opt"), to_one)
    third = flip(packed[2], "ctx", 3)

    product, payloads = project(parts, attention_gain, input_weight, cosine, sine, plan)
    arrived = {shift: lax.ppermute(payloads[shift], "ctx", plan[2][shift]) for shift in HEADS_ORDER}
    passage_parts = [packed[0], one, flip(one, "opt", 1), third, flip(third, "opt", 1)]
    attention = attend(product, arrived, passage_parts, packed[3], plan)
    attention = gathered(attention, "ctx")
    mixed = out_project(attention, output_weight, parts)
    mixed = gathered(mixed, "ctx")
    own_slots, other_slots, mixed_rows, place = route(
        mixed, expert_gain, router_weight.T, attention, slots
    )
    from_x = flip(other_slots, "opt", 2)
    core_own = flip(own_slots, "opt", 1)
    core_x = flip(from_x, "opt", 1)
    own, other, send = experts(
        [own_slots, from_x, core_own, core_x], gate_weight, up_weight, down_weight, tile
    )
    from_core = flip(send, "opt", 1)
    back = flip(merge(other, from_core), "opt", 2)
    own_sum, sends = combine(own, from_core, back, place, ctx_count)
    total = mixed_rows.astype(jnp.float32) + own_sum
    for mask in range(ctx_count - 1, 0, -1):
        total = total + flip(sends[mask - 1], "ctx", mask).astype(jnp.float32)
    return total.astype(jnp.bfloat16)[None]


def takes_fast(mesh, input_weight, output_weight, router_weight, gate_weight):
    ctx_count, opt_count = mesh.shape["ctx"], mesh.shape["opt"]
    devices = ctx_count * opt_count
    return (
        ctx_count == KVH
        and opt_count == 4
        and router_weight.shape[1] == 2 * ctx_count
        and gate_weight.shape[1] == devices * (FF // 2)
        and input_weight.shape[1] % (ctx_count * HD) == 0
        and output_weight.shape[1] % (ctx_count * HD) == 0
    )


def solution(mesh):
    placed = (
        P(("parts", "opt"), "ctx", None),
        P(("parts", "ctx"), None),
        P(("parts", "ctx"), None),
        P(),
        P(),
        P(None, "ctx"),
        P(None, "ctx"),
        P(),
        P(None, ("ctx", "opt")),
        P(None, ("ctx", "opt")),
        P(("ctx", "opt"), None),
        P(("parts", "opt"), "ctx", None),
    )

    def layer(*args):
        fast = takes_fast(mesh, args[5], args[6], args[7], args[8])
        return jax.shard_map(
            fast_shards if fast else general_shards,
            mesh=mesh,
            in_specs=placed,
            out_specs=P(("parts", "opt"), "ctx", None),
            check_vma=False,
        )(*args)

    return layer
```

```python
import jax
import jax.numpy as jnp
from jax import lax
from jax.experimental import pallas as pl
from jax.experimental.pallas import tpu as pltpu
from jax.sharding import PartitionSpec as P


H = 24
KVH = 4
HD = 128
FF = 8192
MOST = 4


EPS = 1e-05
THETA = 1000000.0


def combined_all(x, axis, combine):
    everything = jax.tree.map(
        lambda part, kind: lax.all_gather(part.astype(kind), axis),
        x,
        (jnp.bfloat16, jnp.bfloat16, jnp.bfloat16),
    )

    def take(k):
        return jax.tree.map(lambda part, own: part[k].astype(own.dtype), everything, x)

    return lax.fori_loop(
        1, lax.axis_size(axis), lambda k, so_far: combine(so_far, take(k)), take(0)
    )


def rms_scale(row_data, gain_vector):
    floats = row_data.astype(jnp.float32)
    factor = lax.rsqrt(jnp.mean(floats * floats, axis=-1, keepdims=True) + EPS)
    return (floats * factor * gain_vector).astype(jnp.bfloat16)


def rotate(tile_data, first_head, positions):
    row_count, tile_width = tile_data.shape
    head_count = tile_width // HD
    half_dim = HD // 2
    split_view = tile_data.reshape(row_count, head_count, 2, half_dim)
    inverse = THETA ** (-2.0 * jnp.arange(half_dim, dtype=jnp.float32) / HD)
    angles = positions.astype(jnp.float32)[:, None] * inverse[None, :]
    cosine = jnp.cos(angles)[:, None, :]
    sine_part = jnp.sin(angles)[:, None, :]
    lower_half = split_view[:, :, 0]
    upper_half = split_view[:, :, 1]
    turned = jnp.stack(
        [
            lower_half * cosine - upper_half * sine_part,
            upper_half * cosine + lower_half * sine_part,
        ],
        axis=2,
    )
    rotated_head = first_head + jnp.arange(head_count) < H + KVH
    return jnp.where(rotated_head[None, :, None, None], turned, split_view).reshape(
        row_count, tile_width
    )


def softmax_parts(queries, key_rows, value_rows, key_start, cached):
    key_count = key_rows.shape[0]
    key_heads = key_rows.reshape(key_count, KVH, HD)
    value_heads = value_rows.reshape(key_count, KVH, HD).astype(jnp.float32)
    scores = jnp.einsum(
        "rhgd,khd->hgrk", queries, key_heads, preferred_element_type=jnp.float32
    ) * HD ** (-0.5)
    query_index = jnp.arange(queries.shape[0])
    key_index = jnp.arange(key_count)
    visible = (key_index[None, :] < cached) | (
        key_start + key_index[None, :] - cached <= query_index[:, None]
    )
    scores = jnp.where(visible, scores, -jnp.inf)
    maxima = jnp.max(scores, axis=-1)
    weights = jnp.exp(scores - maxima[..., None])
    totals = jnp.sum(weights, axis=-1)
    summed = jnp.einsum("hgrk,khd->hgrd", weights, value_heads, precision=lax.Precision.HIGHEST)
    return (maxima, totals, summed)


def join_parts(first, second):
    first_max, first_total, first_sum = first
    second_max, second_total, second_sum = second
    larger = jnp.maximum(first_max, second_max)
    first_scale = jnp.exp(first_max - larger)
    second_scale = jnp.exp(second_max - larger)
    return (
        larger,
        first_total * first_scale + second_total * second_scale,
        first_sum * first_scale[..., None] + second_sum * second_scale[..., None],
    )


def general_shards(
    options,
    cache_keys,
    cache_values,
    attention_gain,
    expert_gain,
    input_weight,
    output_weight,
    router_weight,
    gate_weight,
    up_weight,
    down_weight,
    routing,
):
    own_rows = options[0]
    ctx_count = lax.axis_size("ctx")
    ctx_here = lax.axis_index("ctx")
    local_rows = own_rows.shape[0]
    passage = cache_keys.shape[0] * ctx_count
    tile_columns = input_weight.shape[1]
    first_head = ctx_here * (tile_columns // HD)
    normed = rms_scale(own_rows, attention_gain)
    row_piece = lax.all_gather(normed, "ctx", axis=0, tiled=True)
    product = jnp.dot(row_piece, input_weight, preferred_element_type=jnp.float32)
    where_at = passage + jnp.int32(0) + jnp.arange(row_piece.shape[0])
    rotated_tile = rotate(product, first_head, where_at).astype(jnp.bfloat16)
    projected = lax.all_gather(rotated_tile, "ctx", axis=1, tiled=True)
    option_len = projected.shape[0]
    query_width = H * HD
    key_end = (H + KVH) * HD
    queries = projected[:, :query_width].reshape(option_len, KVH, H // KVH, HD)
    option_keys = projected[:, query_width:key_end]
    option_values = projected[:, key_end:]
    own_start = ctx_here * local_rows
    own_keys = lax.dynamic_slice_in_dim(option_keys, own_start, local_rows, 0)
    own_values = lax.dynamic_slice_in_dim(option_values, own_start, local_rows, 0)
    key_rows = jnp.concatenate([cache_keys, own_keys], axis=0)
    value_rows = jnp.concatenate([cache_values, own_values], axis=0)
    local_max, local_total, local_sum = softmax_parts(
        queries, key_rows, value_rows, own_start, cache_keys.shape[0]
    )
    _, totals, summed = combined_all((local_max, local_total, local_sum), "ctx", join_parts)
    attention = (
        (summed / totals[..., None])
        .transpose(2, 0, 1, 3)
        .reshape(option_len, query_width)
        .astype(jnp.bfloat16)
    )
    columns = jnp.dot(attention, output_weight, preferred_element_type=jnp.float32).astype(
        jnp.bfloat16
    )
    attention_out = lax.all_to_all(columns, "ctx", split_axis=0, concat_axis=1, tiled=True)
    mixed_in = (own_rows.astype(jnp.float32) + attention_out.astype(jnp.float32)).astype(
        jnp.bfloat16
    )
    expert_in = rms_scale(mixed_in, expert_gain)
    chosen_ids = routing[0]
    top_count = chosen_ids.shape[1]
    expert_count = router_weight.shape[1]
    logits = jnp.dot(expert_in, router_weight, preferred_element_type=jnp.float32)
    matches = chosen_ids[:, :, None] == jnp.arange(expert_count)[None, None, :]
    picked = jnp.sum(jnp.where(matches, logits[:, None, :], 0.0), axis=-1)
    gate_share = jax.nn.softmax(picked, axis=-1)
    ctx_width = expert_count * FF // ctx_count
    first_target = chosen_ids * FF // ctx_width
    last_target = ((chosen_ids + 1) * FF - 1) // ctx_width
    destination = jnp.arange(ctx_count)
    goes_to = (destination[None, None, :] >= first_target[:, :, None]) & (
        destination[None, None, :] <= last_target[:, :, None]
    )
    flat_goes = goes_to.reshape(local_rows * top_count, ctx_count).astype(jnp.int32)
    slot_index = jnp.cumsum(flat_goes, axis=0) - flat_goes
    slot_count = MOST * max(1, expert_count // ctx_count)
    slot_match = (flat_goes[:, :, None] == 1) & (
        slot_index[:, :, None] == jnp.arange(slot_count)[None, None, :]
    )
    slot_match = slot_match.reshape(local_rows, top_count, ctx_count * slot_count)
    token_slots = jnp.any(slot_match, axis=1).astype(jnp.bfloat16)
    model_width = expert_in.shape[1]
    outgoing = jnp.einsum(
        "rs,rd->sd", token_slots, expert_in, preferred_element_type=jnp.float32
    ).astype(jnp.bfloat16)
    outgoing = outgoing.reshape(ctx_count, slot_count, model_width)
    outgoing_ids = jnp.sum(jnp.where(slot_match, chosen_ids[:, :, None] + 1, 0), axis=(0, 1)) - 1
    outgoing_ids = outgoing_ids.reshape(ctx_count, slot_count)
    arrived, arrived_ids = (
        lax.all_to_all(outgoing, "ctx", split_axis=0, concat_axis=0, tiled=True),
        lax.all_to_all(outgoing_ids, "ctx", split_axis=0, concat_axis=0, tiled=True),
    )
    pooled, pooled_ids = (
        lax.all_gather(arrived, "opt", axis=0, tiled=True),
        lax.all_gather(arrived_ids, "opt", axis=0, tiled=True),
    )
    pooled = pooled.reshape(-1, model_width)
    pooled_ids = pooled_ids.reshape(-1)
    local_width = gate_weight.shape[1]
    opt_count = lax.axis_size("opt")
    column_start = (ctx_here * opt_count + lax.axis_index("opt")) * local_width
    column_expert = (column_start + jnp.arange(local_width)) // FF
    owned_mask = pooled_ids[:, None] == column_expert[None, :]
    gate_part = jnp.dot(pooled, gate_weight, preferred_element_type=jnp.float32)
    up_part = jnp.dot(pooled, up_weight, preferred_element_type=jnp.float32)
    hidden = jnp.where(owned_mask, jax.nn.silu(gate_part) * up_part, 0.0).astype(jnp.bfloat16)
    partial_out = jnp.dot(hidden, down_weight, preferred_element_type=jnp.float32)
    summed_back = lax.psum_scatter(
        partial_out.astype(jnp.bfloat16), "opt", scatter_dimension=0, tiled=True
    ).astype(jnp.float32)
    returned = lax.all_to_all(
        summed_back.reshape(ctx_count, slot_count, model_width).astype(jnp.bfloat16),
        "ctx",
        split_axis=0,
        concat_axis=0,
        tiled=True,
    ).astype(jnp.float32)
    weighting = jnp.sum(jnp.where(slot_match, gate_share[:, :, None], 0.0), axis=1)
    expert_sum = jnp.dot(
        weighting,
        returned.reshape(-1, model_width),
        precision=lax.Precision.HIGHEST,
        preferred_element_type=jnp.float32,
    )
    layer_out = (mixed_in.astype(jnp.float32) + expert_sum).astype(jnp.bfloat16)
    return layer_out[None]


def whole():
    return pl.BlockSpec(memory_space=pltpu.VMEM)


def anywhere():
    return pl.BlockSpec(memory_space=pl.ANY)


def kept(x):
    return pltpu.with_memory_space_constraint(x, pltpu.VMEM)


def flip(x, axis, mask):
    return lax.ppermute(x, axis, [(i, i ^ mask) for i in range(lax.axis_size(axis))])


def gathered(x, axis):
    masks = range(lax.axis_size(axis) - 1, 0, -1)
    return [x] + [flip(x, axis, mask) for mask in masks][::-1]


def aligned(index, size):
    return pl.ds(pl.multiple_of(index * size, size), size)


def cost(flops=0, bytes_accessed=0, transcendentals=0):
    return pl.CostEstimate(
        flops=flops, bytes_accessed=bytes_accessed, transcendentals=transcendentals
    )


def staged():
    return cost(flops=STAGE_FLOPS)


def params(limit):
    return pltpu.CompilerParams(vmem_limit_bytes=limit)


MIB = 1 << 20
STAGE_FLOPS = 8 * 10**9
EXPERT_MIB = 11


class Tiles:
    def __init__(self, source, buffers, sems):
        self.source, self.buffers, self.sems = source, buffers, sems
        self.slots, _, self.width = buffers.shape
        self.count = source.shape[1] // self.width

    def copy(self, i):
        slot = i % self.slots
        return pltpu.make_async_copy(
            self.source.at[:, pl.ds(i * self.width, self.width)],
            self.buffers.at[slot],
            self.sems.at[slot],
        )

    def start(self, i):
        if i < self.count:
            self.copy(i).start()

    def open(self):
        for i in range(self.slots):
            self.start(i)

    def ready(self, i):
        self.copy(i).wait()
        return self.buffers[i % self.slots]


def head_plan(ctx_count, tile_heads):
    per = H // ctx_count
    wanted = [
        [per * c + i for i in range(per)] + [H + c, H + KVH + c] for c in range(ctx_count)
    ]
    sends = {}
    for dst in range(ctx_count):
        for head in wanted[dst]:
            sends.setdefault((head // tile_heads, dst), []).append(head)
    pairs = {}
    for shift in range(1, ctx_count):
        found = [(s, s ^ shift) for s in range(ctx_count)]
        if any(pair in sends for pair in found):
            pairs[shift] = found
    return wanted, sends, pairs


def tables(cosine, sine):
    def kernel(cosine_ref, sine_ref, cosine_out, sine_out):
        cosine_out[...] = cosine_ref[...]
        sine_out[...] = sine_ref[...]

    return pl.pallas_call(
        kernel,
        out_shape=[jax.ShapeDtypeStruct(cosine.shape, cosine.dtype)] * 2,
        in_specs=[whole()] * 2,
        out_specs=[whole()] * 2,
        compiler_params=params(2 * MIB),
        cost_estimate=staged(),
        name="tables",
    )(cosine, sine)


def pack(cache_keys, cache_values, routing, after):
    passage_rows = cache_keys.shape[0]
    top_count, rows = routing.shape
    half = passage_rows // 2

    def kernel(keys_ref, values_ref, routing_ref, after_ref, *refs):
        out_refs, ids_ref = refs[:-1], refs[-1]
        here = lax.axis_index("ctx")
        core = lax.axis_index("opt") % 2
        row = lax.broadcasted_iota(jnp.int32, (rows, rows), 0)
        column = lax.broadcasted_iota(jnp.int32, (rows, rows), 1)
        lane = lax.broadcasted_iota(jnp.int32, (rows, HD), 1)
        numbers = jnp.zeros((rows, HD), jnp.float32)
        for k in range(top_count):
            spread = jnp.where(row == column, routing_ref[k : k + 1, :].astype(jnp.float32), 0.0)
            numbers = numbers + jnp.where(lane == k, jnp.sum(spread, axis=1, keepdims=True), 0.0)
        for ref, who in zip(out_refs, (here, here ^ (1 + core), here ^ 3)):
            count = ref.shape[0]
            start = 0 if count == passage_rows else pl.multiple_of(core * half, half)
            for side, source in enumerate((keys_ref, values_ref)):
                ref[:, side * HD : (side + 1) * HD] = source[pl.ds(start, count), aligned(who, HD)]
        ids_ref[...] = numbers.astype(jnp.bfloat16)

    return pl.pallas_call(
        kernel,
        out_shape=[
            jax.ShapeDtypeStruct((count, 2 * HD), jnp.bfloat16)
            for count in (passage_rows, passage_rows, half)
        ]
        + [jax.ShapeDtypeStruct((rows, HD), jnp.bfloat16)],
        in_specs=[whole()] * 3 + [anywhere()],
        out_specs=[whole()] * 4,
        compiler_params=params(4 * MIB),
        cost_estimate=staged(),
        name="pack",
    )(cache_keys, cache_values, routing, after)


def project(parts, gain, weight, cosine, sine, plan):
    rows, width = parts[0].shape
    ctx_count = len(parts)
    total, columns = rows * ctx_count, weight.shape[1]
    heads = columns // HD
    _, sends, pairs = plan
    shifts = sorted(pairs)
    widths = [max(len(sends.get(pair, [])) for pair in pairs[shift]) * HD for shift in shifts]
    step = 4 * HD

    def kernel(*refs):
        part_refs = refs[:ctx_count]
        gain_ref, weight_ref, cosine_ref, sine_ref, tile_ref = refs[ctx_count : ctx_count + 5]
        payload_refs, normed_ref = refs[ctx_count + 5 : -1], refs[-1]
        here = lax.axis_index("ctx")
        for k in range(ctx_count):
            floats = part_refs[k][...].astype(jnp.float32)
            factor = lax.rsqrt(jnp.mean(floats * floats, axis=-1, keepdims=True) + EPS)
            normed_ref[aligned(here ^ k, rows), :] = floats * factor * gain_ref[...]
        normed = normed_ref[...].astype(jnp.bfloat16)
        for i in range(columns // step):
            product = jnp.dot(
                normed, weight_ref[:, i * step : (i + 1) * step], preferred_element_type=jnp.float32
            )
            for at in range(0, step, HD):
                head = (i * step + at) // HD
                plain = product[:, at : at + HD]
                turned = plain * cosine_ref[...] + pltpu.roll(plain, HD // 2, 1) * sine_ref[...]
                turned = jnp.where(here * heads + head < H + KVH, turned, plain)
                tile_ref[:, head * HD : (head + 1) * HD] = turned.astype(jnp.bfloat16)
        for s in range(ctx_count):

            @pl.when(here == s)
            def _():
                for shift, payload_ref in zip(shifts, payload_refs):
                    for place, head in enumerate(sends.get((s, s ^ shift), [])):
                        local = (head - s * heads) * HD
                        payload_ref[:, place * HD : (place + 1) * HD] = tile_ref[:, local : local + HD]

    out = pl.pallas_call(
        kernel,
        out_shape=[jax.ShapeDtypeStruct((total, n), jnp.bfloat16) for n in [columns] + widths],
        in_specs=[whole()] * (ctx_count + 4),
        out_specs=[whole()] * (1 + len(shifts)),
        scratch_shapes=[pltpu.VMEM((total, width), jnp.float32)],
        compiler_params=params(4 * MIB),
        cost_estimate=cost(bytes_accessed=2 * width * columns),
        name="project",
    )(*parts, gain[None], kept(weight), cosine, sine)
    return out[0], dict(zip(shifts, out[1:]))


def attend(tile, arrived, passage_parts, ids, plan):
    total, rows = tile.shape[0], ids.shape[0]
    ctx_count = lax.axis_size("ctx")
    heads = tile.shape[1] // HD
    wanted, sends, _ = plan
    group = len(wanted[0]) - 2
    shifts = sorted(arrived)

    def kernel(*refs):
        tile_ref = refs[0]
        arrived_refs = dict(zip(shifts, refs[1 : 1 + len(shifts)]))
        passage_refs = refs[1 + len(shifts) : -3]
        numbers_ref, out_ref, mine_ref = refs[-3:]
        here = lax.axis_index("ctx")
        for dst in range(ctx_count):

            @pl.when(here == dst)
            def _():
                for place, head in enumerate(wanted[dst]):
                    src = head // heads
                    if src == dst:
                        block, at = tile_ref, head - src * heads
                    else:
                        block = arrived_refs[dst ^ src]
                        at = sends[(src, dst)].index(head)
                    mine_ref[:, place * HD : (place + 1) * HD] = block[:, at * HD : (at + 1) * HD]

        def part(place):
            return mine_ref[:, place * HD : (place + 1) * HD]

        queries = jnp.concatenate([part(place) for place in range(group)], axis=0)
        keys = [ref[:, :HD] for ref in passage_refs] + [part(group)]
        values = [ref[:, HD:] for ref in passage_refs] + [part(group + 1)]
        scores = []
        for block in keys:
            scores.append(
                lax.dot_general(
                    queries, block, (((1,), (1,)), ((), ())), preferred_element_type=jnp.float32
                )
                * HD ** (-0.5)
            )
        token = lax.broadcasted_iota(jnp.int32, (total, total), 0)
        key = lax.broadcasted_iota(jnp.int32, (total, total), 1)
        bias = jnp.where(key <= token, 0.0, -jnp.inf)
        scores[-1] = scores[-1] + jnp.concatenate([bias] * group, axis=0)
        maxima = jnp.max(scores[0], axis=-1, keepdims=True)
        for block in scores[1:]:
            maxima = jnp.maximum(maxima, jnp.max(block, axis=-1, keepdims=True))
        sums, totals = 0.0, 0.0
        for block, value in zip(scores, values):
            weights = jnp.exp(block - maxima)
            totals = totals + jnp.sum(weights, axis=-1, keepdims=True)
            high = weights.astype(jnp.bfloat16)
            low = (weights - high.astype(jnp.float32)).astype(jnp.bfloat16)
            sums = sums + jnp.dot(high, value, preferred_element_type=jnp.float32)
            sums = sums + jnp.dot(low, value, preferred_element_type=jnp.float32)
        result = (sums / totals).astype(jnp.bfloat16)
        for place in range(group):
            out_ref[:, place * HD : (place + 1) * HD] = result[place * total : (place + 1) * total]
        out_ref[:, group * HD :] = jnp.zeros((total, HD), jnp.bfloat16)
        out_ref[:rows, group * HD :] = numbers_ref[...]

    return pl.pallas_call(
        kernel,
        out_shape=jax.ShapeDtypeStruct((total, (group + 1) * HD), jnp.bfloat16),
        in_specs=[whole()] * (2 + len(shifts) + len(passage_parts)),
        out_specs=whole(),
        scratch_shapes=[pltpu.VMEM((total, (group + 2) * HD), jnp.bfloat16)],
        compiler_params=params(6 * MIB),
        cost_estimate=staged(),
        name="attend",
    )(tile, *[arrived[shift] for shift in shifts], *passage_parts, ids)


def out_project(attention, weight, parts):
    width = attention[0].shape[1] - HD
    rows = parts[0].shape[0]
    ctx_count = len(parts)
    total = rows * ctx_count
    columns = weight.shape[1]

    def kernel(*refs):
        attention_refs, weight_ref = refs[:ctx_count], refs[ctx_count]
        part_refs, (out_ref, raw_ref) = refs[ctx_count + 1 : -2], refs[-2:]
        here = lax.axis_index("ctx")
        for k in range(ctx_count):
            raw_ref[aligned(here ^ k, rows), :] = part_refs[k][:, aligned(here, columns)].astype(jnp.float32)
        product = jnp.zeros((total, columns), jnp.float32)
        for k in range(ctx_count):
            product = product + jnp.dot(
                attention_refs[k][:, :width],
                weight_ref[aligned(here ^ k, width), :],
                preferred_element_type=jnp.float32,
            )
        product = product.astype(jnp.bfloat16).astype(jnp.float32)
        out_ref[...] = (raw_ref[...] + product).astype(jnp.bfloat16)

    return pl.pallas_call(
        kernel,
        out_shape=jax.ShapeDtypeStruct((total, columns), jnp.bfloat16),
        in_specs=[whole()] * (2 * ctx_count + 1),
        out_specs=whole(),
        scratch_shapes=[pltpu.VMEM((total, columns), jnp.float32)],
        compiler_params=params(4 * MIB),
        cost_estimate=cost(flops=STAGE_FLOPS, bytes_accessed=2 * width * ctx_count * columns),
        name="out_project",
    )(*attention, kept(weight), *parts)


def route(mixed, gain, router, id_parts, slots):
    total, columns = mixed[0].shape
    ctx_count = len(mixed)
    rows = total // ctx_count
    width = columns * ctx_count
    expert_count = router.shape[0]

    def kernel(*refs):
        mixed_refs = refs[:ctx_count]
        gain_ref, router_ref = refs[ctx_count : ctx_count + 2]
        id_refs = refs[ctx_count + 2 : 2 * ctx_count + 2]
        own_ref, other_ref, rows_ref, place_ref, full_ref, ids_ref = refs[2 * ctx_count + 2 :]
        here = lax.axis_index("ctx")
        half = lax.axis_index("opt") // 2
        for k in range(ctx_count):
            full_ref[:, aligned(here ^ k, columns)] = mixed_refs[k][...].astype(jnp.float32)
            ids_ref[aligned(here ^ k, rows), :] = id_refs[k][:rows, -HD:].astype(jnp.float32)
        floats = full_ref[...]
        factor = lax.rsqrt(jnp.mean(floats * floats, axis=-1, keepdims=True) + EPS)
        expert_in = (floats * factor * gain_ref[...]).astype(jnp.bfloat16)
        rows_ref[...] = full_ref[aligned(here, rows), :].astype(jnp.bfloat16)
        logits = lax.dot_general(
            expert_in, router_ref[...], (((1,), (1,)), ((), ())), preferred_element_type=jnp.float32
        )
        ids = ids_ref[...].astype(jnp.int32)
        lane = lax.broadcasted_iota(jnp.int32, (total, expert_count), 1)
        first, second = lane == ids[:, 0:1], lane == ids[:, 1:2]
        one = jnp.sum(jnp.where(first, logits, 0.0), axis=1, keepdims=True)
        two = jnp.sum(jnp.where(second, logits, 0.0), axis=1, keepdims=True)
        top = jnp.maximum(one, two)
        one, two = jnp.exp(one - top), jnp.exp(two - top)
        share = jnp.where(first, one / (one + two), 0.0) + jnp.where(second, two / (one + two), 0.0)
        named = jnp.where(first | second, 1.0, 0.0)
        row = lax.broadcasted_iota(jnp.int32, (total, total), 0)
        column = lax.broadcasted_iota(jnp.int32, (total, total), 1)
        earlier = jnp.where(column < row, 1.0, 0.0).astype(jnp.bfloat16)
        rank = jnp.dot(earlier, named.astype(jnp.bfloat16), preferred_element_type=jnp.float32)

        def of(expert, table):
            return jnp.sum(jnp.where(lane == expert, table, 0.0), axis=1, keepdims=True)

        slot = lax.broadcasted_iota(jnp.int32, (total, 2 * slots), 1)
        hits, weights = [], []
        for expert, low in ((here * 2 + half, 0), (here * 2 + 1 - half, slots)):
            place = of(expert, rank).astype(jnp.int32) + low
            inside = (slot >= low) & (slot < low + slots) & (of(expert, named) > 0.5)
            hit = jnp.where(inside & (place == slot), 1.0, 0.0)
            hits.append(hit)
            weights.append(hit * of(expert, share))
        hits = hits[0] + hits[1]
        place_ref[...] = weights[0] + weights[1]
        chosen = lax.dot_general(
            hits.astype(jnp.bfloat16),
            expert_in,
            (((0,), (0,)), ((), ())),
            preferred_element_type=jnp.float32,
        )
        own_ref[...] = chosen[:slots].astype(jnp.bfloat16)
        other_ref[...] = chosen[slots:].astype(jnp.bfloat16)

    return pl.pallas_call(
        kernel,
        out_shape=[
            jax.ShapeDtypeStruct((slots, width), jnp.bfloat16),
            jax.ShapeDtypeStruct((slots, width), jnp.bfloat16),
            jax.ShapeDtypeStruct((rows, width), jnp.bfloat16),
            jax.ShapeDtypeStruct((total, 2 * slots), jnp.float32),
        ],
        in_specs=[whole()] * (2 * ctx_count + 2),
        out_specs=[whole()] * 4,
        scratch_shapes=[
            pltpu.VMEM((total, width), jnp.float32),
            pltpu.VMEM((total, HD), jnp.float32),
        ],
        compiler_params=params(6 * MIB),
        cost_estimate=staged(),
        name="route",
    )(*mixed, gain[None], router, *id_parts)


def experts(blocks, gate, up, down, tile):
    slots, width = blocks[0].shape
    count = slots * len(blocks)
    units = gate.shape[1]
    up_slots = 2
    tall = max(count, 128)

    def kernel(*refs):
        block_refs, refs = refs[: len(blocks)], refs[len(blocks) :]
        gate_ref, up_ref, down_ref, own_ref, other_ref, send_ref = refs[:6]
        rows_ref, hidden_ref, total_ref, ups_ref, up_sems = refs[6:]
        ups = Tiles(up_ref, ups_ref, up_sems)
        ups.open()
        for k in range(tall // slots):
            rows_ref[k * slots : (k + 1) * slots, :] = block_refs[k % len(blocks)][...]

        def add_down(i):
            at = slice(i * tile, (i + 1) * tile)
            hidden = hidden_ref[i % 2]
            for start in range(0, width, 2 * tile):
                cut = slice(start, start + 2 * tile)
                c = jnp.dot(hidden, down_ref[at, cut], preferred_element_type=jnp.float32)[:count]
                total_ref[:, cut] = c if i == 0 else total_ref[:, cut] + c

        def gate_of(i):
            at = slice(i * tile, (i + 1) * tile)
            return jnp.dot(rows_ref[...], gate_ref[:, at], preferred_element_type=jnp.float32)[:count]

        ahead = gate_of(0)
        for i in range(ups.count):
            a = ahead
            if i + 1 < ups.count:
                ahead = gate_of(i + 1)
            b = jnp.dot(rows_ref[...], ups.ready(i), preferred_element_type=jnp.float32)[:count]
            ups.start(i + ups.slots)
            if i > 0:
                add_down(i - 1)
            hidden = (a / (1.0 + jnp.exp(-a)) * b).astype(jnp.bfloat16)
            for k in range(tall // count):
                hidden_ref[i % 2, k * count : (k + 1) * count, :] = hidden
        add_down(ups.count - 1)
        own_ref[...] = total_ref[:slots, :]
        other_ref[...] = total_ref[slots : 2 * slots, :]
        send_ref[...] = total_ref[2 * slots :, :].astype(jnp.bfloat16)

    return pl.pallas_call(
        kernel,
        out_shape=[
            pltpu.VMEM((slots, width), jnp.float32),
            pltpu.VMEM((slots, width), jnp.float32),
            pltpu.VMEM((2 * slots, width), jnp.bfloat16),
        ],
        in_specs=[whole()] * (len(blocks) + 1) + [anywhere(), whole()],
        out_specs=[whole()] * 3,
        scratch_shapes=[
            pltpu.VMEM((tall, width), jnp.bfloat16),
            pltpu.VMEM((2, tall, tile), jnp.bfloat16),
            pltpu.VMEM((count, width), jnp.float32),
            pltpu.VMEM((up_slots, width, tile), jnp.bfloat16),
            pltpu.SemaphoreType.DMA((up_slots,)),
        ],
        compiler_params=params(EXPERT_MIB * MIB),
        cost_estimate=cost(
            flops=6 * count * width * units, bytes_accessed=6 * width * units, transcendentals=count * units
        ),
        name="experts",
    )(*[kept(block) for block in blocks], kept(gate), up, kept(down))


def merge(other, from_core):
    slots, width = other.shape

    def kernel(mine_ref, core_ref, out_ref):
        out_ref[...] = (mine_ref[...] + core_ref[slots:, :].astype(jnp.float32)).astype(jnp.bfloat16)

    return pl.pallas_call(
        kernel,
        out_shape=jax.ShapeDtypeStruct((slots, width), jnp.bfloat16),
        in_specs=[whole()] * 2,
        out_specs=whole(),
        compiler_params=params(4 * MIB),
        name="merge",
    )(kept(other), from_core)


def combine(own, from_core, back, place, ctx_count):
    slots, width = back.shape
    total = place.shape[0]
    rows = total // ctx_count

    def kernel(mine_ref, core_ref, back_ref, place_ref, own_ref, *refs):
        send_refs, spread_ref = refs[:-1], refs[-1]
        here = lax.axis_index("ctx")
        own = mine_ref[...] + core_ref[:slots, :].astype(jnp.float32)
        both = jnp.concatenate([own, back_ref[...].astype(jnp.float32)], axis=0)
        spread_ref[...] = jnp.dot(
            place_ref[...], both, precision=lax.Precision.HIGHEST, preferred_element_type=jnp.float32
        )
        own_ref[...] = spread_ref[aligned(here, rows), :]
        for k, ref in enumerate(send_refs):
            ref[...] = spread_ref[aligned(here ^ (k + 1), rows), :].astype(jnp.bfloat16)

    out = pl.pallas_call(
        kernel,
        out_shape=[jax.ShapeDtypeStruct((rows, width), jnp.float32)]
        + [jax.ShapeDtypeStruct((rows, width), jnp.bfloat16)] * (ctx_count - 1),
        in_specs=[whole()] * 4,
        out_specs=[whole()] * ctx_count,
        scratch_shapes=[pltpu.VMEM((total, width), jnp.float32)],
        compiler_params=params(6 * MIB),
        name="combine",
    )(kept(own), from_core, back, place)
    return out[0], out[1:]


def fast_shards(*args):
    return fast_layer(*args)


def fast_layer(
    options,
    cache_keys,
    cache_values,
    attention_gain,
    expert_gain,
    input_weight,
    output_weight,
    router_weight,
    gate_weight,
    up_weight,
    down_weight,
    routing,
):
    own_rows = options[0]
    local_rows, _ = own_rows.shape
    ctx_count = lax.axis_size("ctx")
    option_len = local_rows * ctx_count
    passage_rows = cache_keys.shape[0]
    passage = passage_rows * ctx_count
    slots = MOST * ctx_count
    plan = head_plan(ctx_count, input_weight.shape[1] // HD)
    tile = 4 * HD

    parts = gathered(own_rows, "ctx")

    half_dim = HD // 2
    inverse = THETA ** (-2.0 * jnp.arange(half_dim, dtype=jnp.float32) / HD)
    positions = (passage + jnp.arange(option_len)).astype(jnp.float32)
    angles = positions[:, None] * inverse[None, :]
    cosine, sine = jnp.cos(angles), jnp.sin(angles)
    cosine = jnp.concatenate([cosine, cosine], axis=1)
    sine = jnp.concatenate([-sine, sine], axis=1)
    cosine, sine = tables(cosine, sine)

    packed = pack(cache_keys, cache_values, routing[0].T, cosine)
    opt_count = lax.axis_size("opt")
    places = [(c, o) for c in range(ctx_count) for o in range(opt_count)]
    to_one = [(c * opt_count + o, (c ^ (1 + o % 2)) * opt_count + o) for c, o in places]
    one = lax.ppermute(packed[1], ("ctx", "opt"), to_one)
    third = flip(packed[2], "ctx", 3)

    product, payloads = project(parts, attention_gain, input_weight, cosine, sine, plan)
    arrived = {}
    for shift in payloads:
        arrived[shift] = lax.ppermute(payloads[shift], "ctx", plan[2][shift])
    passage_parts = [packed[0], one, flip(one, "opt", 1), third, flip(third, "opt", 1)]
    attention = attend(product, arrived, passage_parts, packed[3], plan)
    attention = gathered(attention, "ctx")
    mixed = out_project(attention, output_weight, parts)
    mixed = gathered(mixed, "ctx")
    own_slots, other_slots, mixed_rows, place = route(
        mixed, expert_gain, router_weight.T, attention, slots
    )
    from_x = flip(other_slots, "opt", 2)
    core_own = flip(own_slots, "opt", 1)
    core_x = flip(from_x, "opt", 1)
    own, other, send = experts(
        [own_slots, from_x, core_own, core_x], gate_weight, up_weight, down_weight, tile
    )
    from_core = flip(send, "opt", 1)
    back = flip(merge(other, from_core), "opt", 2)
    own_sum, sends = combine(own, from_core, back, place, ctx_count)
    total = mixed_rows.astype(jnp.float32) + own_sum
    for mask in range(ctx_count - 1, 0, -1):
        total = total + flip(sends[mask - 1], "ctx", mask).astype(jnp.float32)
    return total.astype(jnp.bfloat16)[None]


def takes_fast(mesh, input_weight, output_weight, router_weight, gate_weight):
    ctx_count, opt_count = mesh.shape["ctx"], mesh.shape["opt"]
    devices = ctx_count * opt_count
    return (
        ctx_count == KVH
        and opt_count == 4
        and router_weight.shape[1] == 2 * ctx_count
        and gate_weight.shape[1] == devices * (FF // 2)
        and input_weight.shape[1] % (ctx_count * HD) == 0
        and output_weight.shape[1] % (ctx_count * HD) == 0
    )


def solution(mesh):
    placed = (
        P(("parts", "opt"), "ctx", None),
        P(("parts", "ctx"), None),
        P(("parts", "ctx"), None),
        P(),
        P(),
        P(None, "ctx"),
        P(None, "ctx"),
        P(),
        P(None, ("ctx", "opt")),
        P(None, ("ctx", "opt")),
        P(("ctx", "opt"), None),
        P(("parts", "opt"), "ctx", None),
    )

    def layer(*args):
        fast = takes_fast(mesh, args[5], args[6], args[7], args[8])
        return jax.shard_map(
            fast_shards if fast else general_shards,
            mesh=mesh,
            in_specs=placed,
            out_specs=P(("parts", "opt"), "ctx", None),
            check_vma=False,
        )(*args)

    return layer
```

```python
import jax
import jax.numpy as jnp
from jax import lax
from jax.experimental import pallas as pl
from jax.experimental.pallas import tpu as pltpu
from jax.sharding import PartitionSpec as P


H = 24
KVH = 4
HD = 128
FF = 8192
MOST = 4


EPS = 1e-05
THETA = 1000000.0


def combined_all(x, axis, combine):
    everything = jax.tree.map(
        lambda part, kind: lax.all_gather(part.astype(kind), axis),
        x,
        (jnp.bfloat16, jnp.bfloat16, jnp.bfloat16),
    )

    def take(k):
        return jax.tree.map(lambda part, own: part[k].astype(own.dtype), everything, x)

    return lax.fori_loop(
        1, lax.axis_size(axis), lambda k, so_far: combine(so_far, take(k)), take(0)
    )


def rms_scale(row_data, gain_vector):
    floats = row_data.astype(jnp.float32)
    factor = lax.rsqrt(jnp.mean(floats * floats, axis=-1, keepdims=True) + EPS)
    return (floats * factor * gain_vector).astype(jnp.bfloat16)


def rotate(tile_data, first_head, positions):
    row_count, tile_width = tile_data.shape
    head_count = tile_width // HD
    half_dim = HD // 2
    split_view = tile_data.reshape(row_count, head_count, 2, half_dim)
    inverse = THETA ** (-2.0 * jnp.arange(half_dim, dtype=jnp.float32) / HD)
    angles = positions.astype(jnp.float32)[:, None] * inverse[None, :]
    cosine = jnp.cos(angles)[:, None, :]
    sine_part = jnp.sin(angles)[:, None, :]
    lower_half = split_view[:, :, 0]
    upper_half = split_view[:, :, 1]
    turned = jnp.stack(
        [
            lower_half * cosine - upper_half * sine_part,
            upper_half * cosine + lower_half * sine_part,
        ],
        axis=2,
    )
    rotated_head = first_head + jnp.arange(head_count) < H + KVH
    return jnp.where(rotated_head[None, :, None, None], turned, split_view).reshape(
        row_count, tile_width
    )


def softmax_parts(queries, key_rows, value_rows, key_start, cached):
    key_count = key_rows.shape[0]
    key_heads = key_rows.reshape(key_count, KVH, HD)
    value_heads = value_rows.reshape(key_count, KVH, HD).astype(jnp.float32)
    scores = jnp.einsum(
        "rhgd,khd->hgrk", queries, key_heads, preferred_element_type=jnp.float32
    ) * HD ** (-0.5)
    query_index = jnp.arange(queries.shape[0])
    key_index = jnp.arange(key_count)
    visible = (key_index[None, :] < cached) | (
        key_start + key_index[None, :] - cached <= query_index[:, None]
    )
    scores = jnp.where(visible, scores, -jnp.inf)
    maxima = jnp.max(scores, axis=-1)
    weights = jnp.exp(scores - maxima[..., None])
    totals = jnp.sum(weights, axis=-1)
    summed = jnp.einsum("hgrk,khd->hgrd", weights, value_heads, precision=lax.Precision.HIGHEST)
    return (maxima, totals, summed)


def join_parts(first, second):
    first_max, first_total, first_sum = first
    second_max, second_total, second_sum = second
    larger = jnp.maximum(first_max, second_max)
    first_scale = jnp.exp(first_max - larger)
    second_scale = jnp.exp(second_max - larger)
    return (
        larger,
        first_total * first_scale + second_total * second_scale,
        first_sum * first_scale[..., None] + second_sum * second_scale[..., None],
    )


def general_shards(
    options,
    cache_keys,
    cache_values,
    attention_gain,
    expert_gain,
    input_weight,
    output_weight,
    router_weight,
    gate_weight,
    up_weight,
    down_weight,
    routing,
):
    own_rows = options[0]
    ctx_count = lax.axis_size("ctx")
    ctx_here = lax.axis_index("ctx")
    local_rows = own_rows.shape[0]
    passage = cache_keys.shape[0] * ctx_count
    tile_columns = input_weight.shape[1]
    first_head = ctx_here * (tile_columns // HD)
    normed = rms_scale(own_rows, attention_gain)
    row_piece = lax.all_gather(normed, "ctx", axis=0, tiled=True)
    product = jnp.dot(row_piece, input_weight, preferred_element_type=jnp.float32)
    where_at = passage + jnp.int32(0) + jnp.arange(row_piece.shape[0])
    rotated_tile = rotate(product, first_head, where_at).astype(jnp.bfloat16)
    projected = lax.all_gather(rotated_tile, "ctx", axis=1, tiled=True)
    option_len = projected.shape[0]
    query_width = H * HD
    key_end = (H + KVH) * HD
    queries = projected[:, :query_width].reshape(option_len, KVH, H // KVH, HD)
    option_keys = projected[:, query_width:key_end]
    option_values = projected[:, key_end:]
    own_start = ctx_here * local_rows
    own_keys = lax.dynamic_slice_in_dim(option_keys, own_start, local_rows, 0)
    own_values = lax.dynamic_slice_in_dim(option_values, own_start, local_rows, 0)
    key_rows = jnp.concatenate([cache_keys, own_keys], axis=0)
    value_rows = jnp.concatenate([cache_values, own_values], axis=0)
    local_max, local_total, local_sum = softmax_parts(
        queries, key_rows, value_rows, own_start, cache_keys.shape[0]
    )
    _, totals, summed = combined_all((local_max, local_total, local_sum), "ctx", join_parts)
    attention = (
        (summed / totals[..., None])
        .transpose(2, 0, 1, 3)
        .reshape(option_len, query_width)
        .astype(jnp.bfloat16)
    )
    columns = jnp.dot(attention, output_weight, preferred_element_type=jnp.float32).astype(
        jnp.bfloat16
    )
    attention_out = lax.all_to_all(columns, "ctx", split_axis=0, concat_axis=1, tiled=True)
    mixed_in = (own_rows.astype(jnp.float32) + attention_out.astype(jnp.float32)).astype(
        jnp.bfloat16
    )
    expert_in = rms_scale(mixed_in, expert_gain)
    chosen_ids = routing[0]
    top_count = chosen_ids.shape[1]
    expert_count = router_weight.shape[1]
    logits = jnp.dot(expert_in, router_weight, preferred_element_type=jnp.float32)
    matches = chosen_ids[:, :, None] == jnp.arange(expert_count)[None, None, :]
    picked = jnp.sum(jnp.where(matches, logits[:, None, :], 0.0), axis=-1)
    gate_share = jax.nn.softmax(picked, axis=-1)
    ctx_width = expert_count * FF // ctx_count
    first_target = chosen_ids * FF // ctx_width
    last_target = ((chosen_ids + 1) * FF - 1) // ctx_width
    destination = jnp.arange(ctx_count)
    goes_to = (destination[None, None, :] >= first_target[:, :, None]) & (
        destination[None, None, :] <= last_target[:, :, None]
    )
    flat_goes = goes_to.reshape(local_rows * top_count, ctx_count).astype(jnp.int32)
    slot_index = jnp.cumsum(flat_goes, axis=0) - flat_goes
    slot_count = MOST * max(1, expert_count // ctx_count)
    slot_match = (flat_goes[:, :, None] == 1) & (
        slot_index[:, :, None] == jnp.arange(slot_count)[None, None, :]
    )
    slot_match = slot_match.reshape(local_rows, top_count, ctx_count * slot_count)
    token_slots = jnp.any(slot_match, axis=1).astype(jnp.bfloat16)
    model_width = expert_in.shape[1]
    outgoing = jnp.einsum(
        "rs,rd->sd", token_slots, expert_in, preferred_element_type=jnp.float32
    ).astype(jnp.bfloat16)
    outgoing = outgoing.reshape(ctx_count, slot_count, model_width)
    outgoing_ids = jnp.sum(jnp.where(slot_match, chosen_ids[:, :, None] + 1, 0), axis=(0, 1)) - 1
    outgoing_ids = outgoing_ids.reshape(ctx_count, slot_count)
    arrived, arrived_ids = (
        lax.all_to_all(outgoing, "ctx", split_axis=0, concat_axis=0, tiled=True),
        lax.all_to_all(outgoing_ids, "ctx", split_axis=0, concat_axis=0, tiled=True),
    )
    pooled, pooled_ids = (
        lax.all_gather(arrived, "opt", axis=0, tiled=True),
        lax.all_gather(arrived_ids, "opt", axis=0, tiled=True),
    )
    pooled = pooled.reshape(-1, model_width)
    pooled_ids = pooled_ids.reshape(-1)
    local_width = gate_weight.shape[1]
    opt_count = lax.axis_size("opt")
    column_start = (ctx_here * opt_count + lax.axis_index("opt")) * local_width
    column_expert = (column_start + jnp.arange(local_width)) // FF
    owned_mask = pooled_ids[:, None] == column_expert[None, :]
    gate_part = jnp.dot(pooled, gate_weight, preferred_element_type=jnp.float32)
    up_part = jnp.dot(pooled, up_weight, preferred_element_type=jnp.float32)
    hidden = jnp.where(owned_mask, jax.nn.silu(gate_part) * up_part, 0.0).astype(jnp.bfloat16)
    partial_out = jnp.dot(hidden, down_weight, preferred_element_type=jnp.float32)
    summed_back = lax.psum_scatter(
        partial_out.astype(jnp.bfloat16), "opt", scatter_dimension=0, tiled=True
    ).astype(jnp.float32)
    returned = lax.all_to_all(
        summed_back.reshape(ctx_count, slot_count, model_width).astype(jnp.bfloat16),
        "ctx",
        split_axis=0,
        concat_axis=0,
        tiled=True,
    ).astype(jnp.float32)
    weighting = jnp.sum(jnp.where(slot_match, gate_share[:, :, None], 0.0), axis=1)
    expert_sum = jnp.dot(
        weighting,
        returned.reshape(-1, model_width),
        precision=lax.Precision.HIGHEST,
        preferred_element_type=jnp.float32,
    )
    layer_out = (mixed_in.astype(jnp.float32) + expert_sum).astype(jnp.bfloat16)
    return layer_out[None]


def whole():
    return pl.BlockSpec(memory_space=pltpu.VMEM)


def anywhere():
    return pl.BlockSpec(memory_space=pl.ANY)


def kept(x):
    return pltpu.with_memory_space_constraint(x, pltpu.VMEM)


def flip(x, axis, mask):
    return lax.ppermute(x, axis, [(i, i ^ mask) for i in range(lax.axis_size(axis))])


def gathered(x, axis):
    masks = range(lax.axis_size(axis) - 1, 0, -1)
    return [x] + [flip(x, axis, mask) for mask in masks][::-1]


def aligned(index, size):
    return pl.ds(pl.multiple_of(index * size, size), size)


def cost(flops=0, bytes_accessed=0, transcendentals=0):
    return pl.CostEstimate(
        flops=flops, bytes_accessed=bytes_accessed, transcendentals=transcendentals
    )


def staged():
    return cost(flops=STAGE_FLOPS)


def doubled(x):
    return jnp.concatenate([x] * max(1, 128 // x.shape[0]), axis=0)


def params(limit):
    return pltpu.CompilerParams(vmem_limit_bytes=limit)


MIB = 1 << 20
STAGE_FLOPS = 6 * 10**9
EXPERT_MIB = 11


class Tiles:
    def __init__(self, source, buffers, sems):
        self.source, self.buffers, self.sems = source, buffers, sems
        self.slots, _, self.width = buffers.shape
        self.count = source.shape[1] // self.width

    def copy(self, i):
        slot = i % self.slots
        return pltpu.make_async_copy(
            self.source.at[:, pl.ds(i * self.width, self.width)],
            self.buffers.at[slot],
            self.sems.at[slot],
        )

    def start(self, i):
        if i < self.count:
            self.copy(i).start()

    def open(self):
        for i in range(self.slots):
            self.start(i)

    def ready(self, i):
        self.copy(i).wait()
        return self.buffers[i % self.slots]


def head_plan(ctx_count, tile_heads):
    per = H // ctx_count
    wanted = [
        [per * c + i for i in range(per)] + [H + c, H + KVH + c] for c in range(ctx_count)
    ]
    sends = {}
    for dst in range(ctx_count):
        for head in wanted[dst]:
            sends.setdefault((head // tile_heads, dst), []).append(head)
    pairs = {}
    for shift in range(1, ctx_count):
        found = [(s, s ^ shift) for s in range(ctx_count)]
        if any(pair in sends for pair in found):
            pairs[shift] = found
    return wanted, sends, pairs


def tables(cosine, sine):
    def kernel(cosine_ref, sine_ref, cosine_out, sine_out):
        cosine_out[...] = cosine_ref[...]
        sine_out[...] = sine_ref[...]

    return pl.pallas_call(
        kernel,
        out_shape=[jax.ShapeDtypeStruct(cosine.shape, cosine.dtype)] * 2,
        in_specs=[whole()] * 2,
        out_specs=[whole()] * 2,
        compiler_params=params(2 * MIB),
        cost_estimate=staged(),
        name="tables",
    )(cosine, sine)


def pack(cache_keys, cache_values, routing, after):
    passage_rows = cache_keys.shape[0]
    top_count, rows = routing.shape
    half = passage_rows // 2

    def kernel(keys_ref, values_ref, routing_ref, after_ref, *refs):
        out_refs, ids_ref = refs[:-1], refs[-1]
        here = lax.axis_index("ctx")
        core = lax.axis_index("opt") % 2
        row = lax.broadcasted_iota(jnp.int32, (rows, rows), 0)
        column = lax.broadcasted_iota(jnp.int32, (rows, rows), 1)
        lane = lax.broadcasted_iota(jnp.int32, (rows, HD), 1)
        numbers = jnp.zeros((rows, HD), jnp.float32)
        for k in range(top_count):
            spread = jnp.where(row == column, routing_ref[k : k + 1, :].astype(jnp.float32), 0.0)
            numbers = numbers + jnp.where(lane == k, jnp.sum(spread, axis=1, keepdims=True), 0.0)
        for ref, who in zip(out_refs, (here, here ^ (1 + core), here ^ 3)):
            count = ref.shape[0]
            start = 0 if count == passage_rows else pl.multiple_of(core * half, half)
            for side, source in enumerate((keys_ref, values_ref)):
                ref[:, side * HD : (side + 1) * HD] = source[pl.ds(start, count), aligned(who, HD)]
        ids_ref[...] = numbers.astype(jnp.bfloat16)

    return pl.pallas_call(
        kernel,
        out_shape=[
            jax.ShapeDtypeStruct((count, 2 * HD), jnp.bfloat16)
            for count in (passage_rows, passage_rows, half)
        ]
        + [jax.ShapeDtypeStruct((rows, HD), jnp.bfloat16)],
        in_specs=[whole()] * 3 + [anywhere()],
        out_specs=[whole()] * 4,
        compiler_params=params(4 * MIB),
        cost_estimate=staged(),
        name="pack",
    )(cache_keys, cache_values, routing, after)


def project(parts, gain, weight, cosine, sine, plan):
    rows, width = parts[0].shape
    ctx_count = len(parts)
    total, columns = rows * ctx_count, weight.shape[1]
    heads = columns // HD
    _, sends, pairs = plan
    shifts = sorted(pairs)
    widths = [max(len(sends.get(pair, [])) for pair in pairs[shift]) * HD for shift in shifts]
    step = 4 * HD

    def kernel(*refs):
        part_refs = refs[:ctx_count]
        gain_ref, weight_ref, cosine_ref, sine_ref, tile_ref = refs[ctx_count : ctx_count + 5]
        payload_refs, normed_ref = refs[ctx_count + 5 : -1], refs[-1]
        here = lax.axis_index("ctx")
        for k in range(ctx_count):
            floats = part_refs[k][...].astype(jnp.float32)
            factor = lax.rsqrt(jnp.mean(floats * floats, axis=-1, keepdims=True) + EPS)
            normed_ref[aligned(here ^ k, rows), :] = floats * factor * gain_ref[...]
        normed = doubled(normed_ref[...].astype(jnp.bfloat16))
        for i in range(columns // step):
            product = jnp.dot(
                normed, weight_ref[:, i * step : (i + 1) * step], preferred_element_type=jnp.float32
            )[:total]
            for at in range(0, step, HD):
                head = (i * step + at) // HD
                plain = product[:, at : at + HD]
                turned = plain * cosine_ref[...] + pltpu.roll(plain, HD // 2, 1) * sine_ref[...]
                turned = jnp.where(here * heads + head < H + KVH, turned, plain)
                tile_ref[:, head * HD : (head + 1) * HD] = turned.astype(jnp.bfloat16)
        for s in range(ctx_count):

            @pl.when(here == s)
            def _():
                for shift, payload_ref in zip(shifts, payload_refs):
                    for place, head in enumerate(sends.get((s, s ^ shift), [])):
                        local = (head - s * heads) * HD
                        payload_ref[:, place * HD : (place + 1) * HD] = tile_ref[:, local : local + HD]

    out = pl.pallas_call(
        kernel,
        out_shape=[jax.ShapeDtypeStruct((total, n), jnp.bfloat16) for n in [columns] + widths],
        in_specs=[whole()] * (ctx_count + 4),
        out_specs=[whole()] * (1 + len(shifts)),
        scratch_shapes=[pltpu.VMEM((total, width), jnp.float32)],
        compiler_params=params(4 * MIB),
        cost_estimate=cost(bytes_accessed=2 * width * columns),
        name="project",
    )(*parts, gain[None], kept(weight), cosine, sine)
    return out[0], dict(zip(shifts, out[1:]))


def attend(tile, arrived, passage_parts, ids, plan):
    total, rows = tile.shape[0], ids.shape[0]
    ctx_count = lax.axis_size("ctx")
    heads = tile.shape[1] // HD
    wanted, sends, _ = plan
    group = len(wanted[0]) - 2
    shifts = sorted(arrived)

    def kernel(*refs):
        tile_ref = refs[0]
        arrived_refs = dict(zip(shifts, refs[1 : 1 + len(shifts)]))
        passage_refs = refs[1 + len(shifts) : -3]
        numbers_ref, out_ref, mine_ref = refs[-3:]
        here = lax.axis_index("ctx")
        for dst in range(ctx_count):

            @pl.when(here == dst)
            def _():
                for place, head in enumerate(wanted[dst]):
                    src = head // heads
                    if src == dst:
                        block, at = tile_ref, head - src * heads
                    else:
                        block = arrived_refs[dst ^ src]
                        at = sends[(src, dst)].index(head)
                    mine_ref[:, place * HD : (place + 1) * HD] = block[:, at * HD : (at + 1) * HD]

        def part(place):
            return mine_ref[:, place * HD : (place + 1) * HD]

        queries = jnp.concatenate([part(place) for place in range(group)], axis=0)
        keys = [ref[:, :HD] for ref in passage_refs] + [part(group)]
        values = [ref[:, HD:] for ref in passage_refs] + [part(group + 1)]
        scores = []
        for block in keys:
            scores.append(
                lax.dot_general(
                    queries, block, (((1,), (1,)), ((), ())), preferred_element_type=jnp.float32
                )
                * HD ** (-0.5)
            )
        token = lax.broadcasted_iota(jnp.int32, (total, total), 0)
        key = lax.broadcasted_iota(jnp.int32, (total, total), 1)
        bias = jnp.where(key <= token, 0.0, -jnp.inf)
        scores[-1] = scores[-1] + jnp.concatenate([bias] * group, axis=0)
        maxima = jnp.max(scores[0], axis=-1, keepdims=True)
        for block in scores[1:]:
            maxima = jnp.maximum(maxima, jnp.max(block, axis=-1, keepdims=True))
        sums, totals = 0.0, 0.0
        for block, value in zip(scores, values):
            weights = jnp.exp(block - maxima)
            totals = totals + jnp.sum(weights, axis=-1, keepdims=True)
            high = weights.astype(jnp.bfloat16)
            low = (weights - high.astype(jnp.float32)).astype(jnp.bfloat16)
            sums = sums + jnp.dot(high, value, preferred_element_type=jnp.float32)
            sums = sums + jnp.dot(low, value, preferred_element_type=jnp.float32)
        result = (sums / totals).astype(jnp.bfloat16)
        for place in range(group):
            out_ref[:, place * HD : (place + 1) * HD] = result[place * total : (place + 1) * total]
        out_ref[:, group * HD :] = jnp.zeros((total, HD), jnp.bfloat16)
        out_ref[:rows, group * HD :] = numbers_ref[...]

    return pl.pallas_call(
        kernel,
        out_shape=jax.ShapeDtypeStruct((total, (group + 1) * HD), jnp.bfloat16),
        in_specs=[whole()] * (2 + len(shifts) + len(passage_parts)),
        out_specs=whole(),
        scratch_shapes=[pltpu.VMEM((total, (group + 2) * HD), jnp.bfloat16)],
        compiler_params=params(6 * MIB),
        cost_estimate=staged(),
        name="attend",
    )(tile, *[arrived[shift] for shift in shifts], *passage_parts, ids)


def out_project(attention, weight, parts):
    width = attention[0].shape[1] - HD
    rows = parts[0].shape[0]
    ctx_count = len(parts)
    total = rows * ctx_count
    columns = weight.shape[1]

    def kernel(*refs):
        attention_refs, weight_ref = refs[:ctx_count], refs[ctx_count]
        part_refs, (out_ref, raw_ref) = refs[ctx_count + 1 : -2], refs[-2:]
        here = lax.axis_index("ctx")
        for k in range(ctx_count):
            raw_ref[aligned(here ^ k, rows), :] = part_refs[k][:, aligned(here, columns)].astype(jnp.float32)
        product = jnp.zeros((total, columns), jnp.float32)
        for k in range(ctx_count):
            product = product + jnp.dot(
                doubled(attention_refs[k][:, :width]),
                weight_ref[aligned(here ^ k, width), :],
                preferred_element_type=jnp.float32,
            )[:total]
        product = product.astype(jnp.bfloat16).astype(jnp.float32)
        out_ref[...] = (raw_ref[...] + product).astype(jnp.bfloat16)

    return pl.pallas_call(
        kernel,
        out_shape=jax.ShapeDtypeStruct((total, columns), jnp.bfloat16),
        in_specs=[whole()] * (2 * ctx_count + 1),
        out_specs=whole(),
        scratch_shapes=[pltpu.VMEM((total, columns), jnp.float32)],
        compiler_params=params(4 * MIB),
        cost_estimate=cost(flops=STAGE_FLOPS, bytes_accessed=2 * width * ctx_count * columns),
        name="out_project",
    )(*attention, kept(weight), *parts)


def route(mixed, gain, router, id_parts, slots):
    total, columns = mixed[0].shape
    ctx_count = len(mixed)
    rows = total // ctx_count
    width = columns * ctx_count
    expert_count = router.shape[0]

    def kernel(*refs):
        mixed_refs = refs[:ctx_count]
        gain_ref, router_ref = refs[ctx_count : ctx_count + 2]
        id_refs = refs[ctx_count + 2 : 2 * ctx_count + 2]
        own_ref, other_ref, rows_ref, place_ref, full_ref, ids_ref = refs[2 * ctx_count + 2 :]
        here = lax.axis_index("ctx")
        half = lax.axis_index("opt") // 2
        for k in range(ctx_count):
            full_ref[:, aligned(here ^ k, columns)] = mixed_refs[k][...].astype(jnp.float32)
            ids_ref[aligned(here ^ k, rows), :] = id_refs[k][:rows, -HD:].astype(jnp.float32)
        floats = full_ref[...]
        factor = lax.rsqrt(jnp.mean(floats * floats, axis=-1, keepdims=True) + EPS)
        expert_in = (floats * factor * gain_ref[...]).astype(jnp.bfloat16)
        rows_ref[...] = full_ref[aligned(here, rows), :].astype(jnp.bfloat16)
        logits = lax.dot_general(
            expert_in, router_ref[...], (((1,), (1,)), ((), ())), preferred_element_type=jnp.float32
        )
        ids = ids_ref[...].astype(jnp.int32)
        lane = lax.broadcasted_iota(jnp.int32, (total, expert_count), 1)
        first, second = lane == ids[:, 0:1], lane == ids[:, 1:2]
        one = jnp.sum(jnp.where(first, logits, 0.0), axis=1, keepdims=True)
        two = jnp.sum(jnp.where(second, logits, 0.0), axis=1, keepdims=True)
        top = jnp.maximum(one, two)
        one, two = jnp.exp(one - top), jnp.exp(two - top)
        share = jnp.where(first, one / (one + two), 0.0) + jnp.where(second, two / (one + two), 0.0)
        named = jnp.where(first | second, 1.0, 0.0)
        row = lax.broadcasted_iota(jnp.int32, (total, total), 0)
        column = lax.broadcasted_iota(jnp.int32, (total, total), 1)
        earlier = jnp.where(column < row, 1.0, 0.0).astype(jnp.bfloat16)
        rank = jnp.dot(earlier, named.astype(jnp.bfloat16), preferred_element_type=jnp.float32)

        def of(expert, table):
            return jnp.sum(jnp.where(lane == expert, table, 0.0), axis=1, keepdims=True)

        slot = lax.broadcasted_iota(jnp.int32, (total, 2 * slots), 1)
        hits, weights = [], []
        for expert, low in ((here * 2 + half, 0), (here * 2 + 1 - half, slots)):
            place = of(expert, rank).astype(jnp.int32) + low
            inside = (slot >= low) & (slot < low + slots) & (of(expert, named) > 0.5)
            hit = jnp.where(inside & (place == slot), 1.0, 0.0)
            hits.append(hit)
            weights.append(hit * of(expert, share))
        hits = hits[0] + hits[1]
        place_ref[...] = weights[0] + weights[1]
        chosen = lax.dot_general(
            hits.astype(jnp.bfloat16),
            expert_in,
            (((0,), (0,)), ((), ())),
            preferred_element_type=jnp.float32,
        )
        own_ref[...] = chosen[:slots].astype(jnp.bfloat16)
        other_ref[...] = chosen[slots:].astype(jnp.bfloat16)

    return pl.pallas_call(
        kernel,
        out_shape=[
            jax.ShapeDtypeStruct((slots, width), jnp.bfloat16),
            jax.ShapeDtypeStruct((slots, width), jnp.bfloat16),
            jax.ShapeDtypeStruct((rows, width), jnp.bfloat16),
            jax.ShapeDtypeStruct((total, 2 * slots), jnp.float32),
        ],
        in_specs=[whole()] * (2 * ctx_count + 2),
        out_specs=[whole()] * 4,
        scratch_shapes=[
            pltpu.VMEM((total, width), jnp.float32),
            pltpu.VMEM((total, HD), jnp.float32),
        ],
        compiler_params=params(6 * MIB),
        cost_estimate=staged(),
        name="route",
    )(*mixed, gain[None], router, *id_parts)


def experts(blocks, gate, up, down, tile):
    slots, width = blocks[0].shape
    count = slots * len(blocks)
    units = gate.shape[1]
    up_slots = 2
    tall = max(count, 128)

    def kernel(*refs):
        block_refs, refs = refs[: len(blocks)], refs[len(blocks) :]
        gate_ref, up_ref, down_ref, own_ref, other_ref, send_ref = refs[:6]
        rows_ref, hidden_ref, total_ref, ups_ref, up_sems = refs[6:]
        ups = Tiles(up_ref, ups_ref, up_sems)
        ups.open()
        for k in range(tall // slots):
            rows_ref[k * slots : (k + 1) * slots, :] = block_refs[k % len(blocks)][...]

        def add_down(i):
            at = slice(i * tile, (i + 1) * tile)
            hidden = hidden_ref[i % 2]
            for start in range(0, width, 2 * tile):
                cut = slice(start, start + 2 * tile)
                c = jnp.dot(hidden, down_ref[at, cut], preferred_element_type=jnp.float32)[:count]
                total_ref[:, cut] = c if i == 0 else total_ref[:, cut] + c

        def gate_of(i):
            at = slice(i * tile, (i + 1) * tile)
            return jnp.dot(rows_ref[...], gate_ref[:, at], preferred_element_type=jnp.float32)[:count]

        ahead = gate_of(0)
        for i in range(ups.count):
            a = ahead
            if i + 1 < ups.count:
                ahead = gate_of(i + 1)
            b = jnp.dot(rows_ref[...], ups.ready(i), preferred_element_type=jnp.float32)[:count]
            ups.start(i + ups.slots)
            if i > 0:
                add_down(i - 1)
            hidden = (a / (1.0 + jnp.exp(-a)) * b).astype(jnp.bfloat16)
            for k in range(tall // count):
                hidden_ref[i % 2, k * count : (k + 1) * count, :] = hidden
        add_down(ups.count - 1)
        own_ref[...] = total_ref[:slots, :]
        other_ref[...] = total_ref[slots : 2 * slots, :]
        send_ref[...] = total_ref[2 * slots :, :].astype(jnp.bfloat16)

    return pl.pallas_call(
        kernel,
        out_shape=[
            pltpu.VMEM((slots, width), jnp.float32),
            pltpu.VMEM((slots, width), jnp.float32),
            pltpu.VMEM((2 * slots, width), jnp.bfloat16),
        ],
        in_specs=[whole()] * (len(blocks) + 1) + [anywhere(), whole()],
        out_specs=[whole()] * 3,
        scratch_shapes=[
            pltpu.VMEM((tall, width), jnp.bfloat16),
            pltpu.VMEM((2, tall, tile), jnp.bfloat16),
            pltpu.VMEM((count, width), jnp.float32),
            pltpu.VMEM((up_slots, width, tile), jnp.bfloat16),
            pltpu.SemaphoreType.DMA((up_slots,)),
        ],
        compiler_params=params(EXPERT_MIB * MIB),
        cost_estimate=cost(
            flops=6 * count * width * units, bytes_accessed=6 * width * units, transcendentals=count * units
        ),
        name="experts",
    )(*[kept(block) for block in blocks], kept(gate), up, kept(down))


def merge(other, from_core):
    slots, width = other.shape

    def kernel(mine_ref, core_ref, out_ref):
        out_ref[...] = (mine_ref[...] + core_ref[slots:, :].astype(jnp.float32)).astype(jnp.bfloat16)

    return pl.pallas_call(
        kernel,
        out_shape=jax.ShapeDtypeStruct((slots, width), jnp.bfloat16),
        in_specs=[whole()] * 2,
        out_specs=whole(),
        compiler_params=params(4 * MIB),
        name="merge",
    )(kept(other), from_core)


def combine(own, from_core, back, place, ctx_count):
    slots, width = back.shape
    total = place.shape[0]
    rows = total // ctx_count

    def kernel(mine_ref, core_ref, back_ref, place_ref, own_ref, *refs):
        send_refs, spread_ref = refs[:-1], refs[-1]
        here = lax.axis_index("ctx")
        own = mine_ref[...] + core_ref[:slots, :].astype(jnp.float32)
        both = jnp.concatenate([own, back_ref[...].astype(jnp.float32)], axis=0)
        spread_ref[...] = jnp.dot(
            place_ref[...], both, precision=lax.Precision.HIGHEST, preferred_element_type=jnp.float32
        )
        own_ref[...] = spread_ref[aligned(here, rows), :]
        for k, ref in enumerate(send_refs):
            ref[...] = spread_ref[aligned(here ^ (k + 1), rows), :].astype(jnp.bfloat16)

    out = pl.pallas_call(
        kernel,
        out_shape=[jax.ShapeDtypeStruct((rows, width), jnp.float32)]
        + [jax.ShapeDtypeStruct((rows, width), jnp.bfloat16)] * (ctx_count - 1),
        in_specs=[whole()] * 4,
        out_specs=[whole()] * ctx_count,
        scratch_shapes=[pltpu.VMEM((total, width), jnp.float32)],
        compiler_params=params(6 * MIB),
        name="combine",
    )(kept(own), from_core, back, place)
    return out[0], out[1:]


def fast_shards(*args):
    return fast_layer(*args)


def fast_layer(
    options,
    cache_keys,
    cache_values,
    attention_gain,
    expert_gain,
    input_weight,
    output_weight,
    router_weight,
    gate_weight,
    up_weight,
    down_weight,
    routing,
):
    own_rows = options[0]
    local_rows, _ = own_rows.shape
    ctx_count = lax.axis_size("ctx")
    option_len = local_rows * ctx_count
    passage_rows = cache_keys.shape[0]
    passage = passage_rows * ctx_count
    slots = MOST * ctx_count
    plan = head_plan(ctx_count, input_weight.shape[1] // HD)
    tile = 4 * HD

    parts = gathered(own_rows, "ctx")

    half_dim = HD // 2
    inverse = THETA ** (-2.0 * jnp.arange(half_dim, dtype=jnp.float32) / HD)
    positions = (passage + jnp.arange(option_len)).astype(jnp.float32)
    angles = positions[:, None] * inverse[None, :]
    cosine, sine = jnp.cos(angles), jnp.sin(angles)
    cosine = jnp.concatenate([cosine, cosine], axis=1)
    sine = jnp.concatenate([-sine, sine], axis=1)
    cosine, sine = tables(cosine, sine)

    packed = pack(cache_keys, cache_values, routing[0].T, cosine)
    opt_count = lax.axis_size("opt")
    places = [(c, o) for c in range(ctx_count) for o in range(opt_count)]
    to_one = [(c * opt_count + o, (c ^ (1 + o % 2)) * opt_count + o) for c, o in places]
    one = lax.ppermute(packed[1], ("ctx", "opt"), to_one)
    third = flip(packed[2], "ctx", 3)

    product, payloads = project(parts, attention_gain, input_weight, cosine, sine, plan)
    arrived = {}
    for shift in payloads:
        arrived[shift] = lax.ppermute(payloads[shift], "ctx", plan[2][shift])
    passage_parts = [packed[0], one, flip(one, "opt", 1), third, flip(third, "opt", 1)]
    attention = attend(product, arrived, passage_parts, packed[3], plan)
    attention = gathered(attention, "ctx")
    mixed = out_project(attention, output_weight, parts)
    mixed = gathered(mixed, "ctx")
    own_slots, other_slots, mixed_rows, place = route(
        mixed, expert_gain, router_weight.T, attention, slots
    )
    from_x = flip(other_slots, "opt", 2)
    core_own = flip(own_slots, "opt", 1)
    core_x = flip(from_x, "opt", 1)
    own, other, send = experts(
        [own_slots, from_x, core_own, core_x], gate_weight, up_weight, down_weight, tile
    )
    from_core = flip(send, "opt", 1)
    back = flip(merge(other, from_core), "opt", 2)
    own_sum, sends = combine(own, from_core, back, place, ctx_count)
    total = mixed_rows.astype(jnp.float32) + own_sum
    for mask in range(ctx_count - 1, 0, -1):
        total = total + flip(sends[mask - 1], "ctx", mask).astype(jnp.float32)
    return total.astype(jnp.bfloat16)[None]


def takes_fast(mesh, input_weight, output_weight, router_weight, gate_weight):
    ctx_count, opt_count = mesh.shape["ctx"], mesh.shape["opt"]
    devices = ctx_count * opt_count
    return (
        ctx_count == KVH
        and opt_count == 4
        and router_weight.shape[1] == 2 * ctx_count
        and gate_weight.shape[1] == devices * (FF // 2)
        and input_weight.shape[1] % (ctx_count * HD) == 0
        and output_weight.shape[1] % (ctx_count * HD) == 0
    )


def solution(mesh):
    placed = (
        P(("parts", "opt"), "ctx", None),
        P(("parts", "ctx"), None),
        P(("parts", "ctx"), None),
        P(),
        P(),
        P(None, "ctx"),
        P(None, "ctx"),
        P(),
        P(None, ("ctx", "opt")),
        P(None, ("ctx", "opt")),
        P(("ctx", "opt"), None),
        P(("parts", "opt"), "ctx", None),
    )

    def layer(*args):
        fast = takes_fast(mesh, args[5], args[6], args[7], args[8])
        return jax.shard_map(
            fast_shards if fast else general_shards,
            mesh=mesh,
            in_specs=placed,
            out_specs=P(("parts", "opt"), "ctx", None),
            check_vma=False,
        )(*args)

    return layer
```
